32 devices in a mesh: ctx: 16 (over z, y, core), wsh: 2 (over x).
Axes of the slice: x: 2, y: 2, z: 4, core: 2. Of those that a mesh axis runs over, the one named last changes fastest.
Arguments:
- tokens: bfloat16 [4, 4096, 768], P('wsh', 'ctx'), may hold values from -6 to 6
- first_values: bfloat16 [4, 4096, 384], P('wsh', 'ctx'), may hold values from -6 to 6
- teacher: bfloat16 [4, 4096, 768], P('wsh', 'ctx'), may hold values from -20 to 20
- segment_ids: int32 [4, 4096], P('wsh'), may hold values from 0 to 3, never falling along the last dimension, each value on 1 to 2048 neighbouring positions
- lengths: int32 [4], P('wsh'), may hold values from 2049 to 4096, as said below
- ln1_gain: bfloat16 [768], P('wsh'), may hold values from 0.5 to 1.5
- ln1_bias: bfloat16 [768], P('wsh'), may hold values from -1 to 1
- w_qkv: bfloat16 [768, 1920], P('wsh'), may hold values from -0.21875 to 0.21875
- qv_bias: bfloat16 [1152], P('wsh'), may hold values from -1 to 1
- w_out: bfloat16 [768, 768], P('wsh'), may hold values from -1.75 to 1.75
- b_out: bfloat16 [768], P('wsh'), may hold values from -1 to 1
- ln2_gain: bfloat16 [768], P('wsh'), may hold values from 0.5 to 1.5
- ln2_bias: bfloat16 [768], P('wsh'), may hold values from -1 to 1
- w_fc: bfloat16 [768, 3072], P('wsh'), may hold values from -0.21875 to 0.21875
- b_fc: bfloat16 [3072], P('wsh'), may hold values from -1 to 1
- w_proj: bfloat16 [3072, 768], P('wsh'), may hold values from -0.109375 to 0.109375
- b_proj: bfloat16 [768], P('wsh'), may hold values from -1 to 1
Outputs:
- loss: float32 [], replicated
- output: bfloat16 [4, 4096, 768], P('wsh', 'ctx')
- grad_tokens: float32 [4, 4096, 768], P('wsh', 'ctx')
- grad_first: float32 [4, 4096, 384], P('wsh', 'ctx')
- grad_ln1_gain: float32 [768], P('wsh')
- grad_ln1_bias: float32 [768], P('wsh')
- grad_w_qkv: float32 [768, 1920], P('wsh')
- grad_qv_bias: float32 [1152], P('wsh')
- grad_w_out: float32 [768, 768], P('wsh')
- grad_b_out: float32 [768], P('wsh')
- grad_ln2_gain: float32 [768], P('wsh')
- grad_ln2_bias: float32 [768], P('wsh')
- grad_w_fc: float32 [768, 3072], P('wsh')
- grad_b_fc: float32 [3072], P('wsh')
- grad_w_proj: float32 [3072, 768], P('wsh')
- grad_b_proj: float32 [768], P('wsh')
The draws below stay inside these ranges and needn't reach their ends.
Inputs may be any that keep to these rules, and one draw needn't show every extreme that they name: `segment_ids`: along each sequence the ids never fall; every document (run of one id) has 1 to 2048 tokens, and some document has exactly 2048. `lengths`: in each group of 2 consecutive sequences, one is valid in full.
All inputs are finite; a program needn't handle non-finite values.
Results may differ from the reference program's by a relative error of at most 0.013.
Values may be sent and summed in bfloat16 or wider, within the bound.
A program may use at most 192 MiB of HBM per device.

```python
import math
import jax
import jax.numpy as jnp
import numpy as np
from jax import lax

D = 768
HEADS = 12
HEAD = 64
FF = 3072
SEQS = 2
DOC_MAX = 2048
VW = 384
SEQ_LEN = 4096
SEQ_ALL = 4
SEGS = 4


def draw_teacher(key, part):
    position = jnp.arange(SEQ_LEN, dtype=jnp.float32) / SEQ_LEN
    base = jnp.clip(jax.random.normal(key, (SEQ_ALL, SEQ_LEN, D), jnp.float32), -6.0, 6.0)
    return (base * (1.0 + 2.0 * position)[None, :, None]).astype(jnp.bfloat16)


def draw_lengths(key, part):
    removed = jax.random.randint(jax.random.fold_in(key, 1), (SEQ_ALL,), 0, SEQ_LEN // 2, dtype=jnp.int32)
    chosen = jax.random.randint(jax.random.fold_in(key, 2), (SEQ_ALL // SEQS,), 0, SEQS, dtype=jnp.int32)
    index = jnp.arange(SEQ_ALL, dtype=jnp.int32)
    full = index % SEQS == jnp.repeat(chosen, SEQS)
    removed = jnp.where(full, 0, removed)
    return (SEQ_LEN - removed).astype(jnp.int32)


def shard_levels(key, shape, shards, least, largest):
    def one(axis_at, blocks):
        heights = jax.random.uniform(jax.random.fold_in(jax.random.fold_in(key, 6), axis_at), (blocks,), jnp.float32, least / len(shards), largest / len(shards))
        return jnp.repeat(jnp.exp(heights), shape[axis_at] // blocks).reshape((-1,) + (1,) * (len(shape) - axis_at - 1))

    level = one(*shards[0])
    for cut in shards[1:]:
        level = level * one(*cut)
    return level


def length_profile(number_of, total, limit, skew):
    weights = [(1 << 20) // math.isqrt(rank ** skew) + 1 for rank in range(2, number_of + 1)]
    spare, given = total - limit - (number_of - 1), [1] * (number_of - 1)
    while spare > 0:
        movable = [i for i in range(number_of - 1) if given[i] < limit]
        mass, budget = sum([weights[i] for i in movable]), spare
        for i in movable:
            more = min(limit - given[i], max(1, budget * weights[i] // mass), spare)
            given[i] = given[i] + more
            spare = spare - more
    return np.array([limit] + given)


def ragged(rng, count, total, reach, slope):
    if count == 2:
        one = jax.random.randint(rng, (), max(1, total - reach), min(reach, total - 1) + 1)
        return jnp.stack([one, total - one])
    tallies = jnp.asarray(length_profile(count, total, reach, slope), jnp.int32)
    couples = (count - 1) // 2
    giver, sink = tallies[1:1 + 2 * couples:2], tallies[2:2 + 2 * couples:2]
    room = jnp.minimum(giver - 1, reach - sink)
    passed = jax.random.randint(jax.random.fold_in(rng, 1), (couples,), 0, 1 << 20) % (room + 1)
    tallies = tallies.at[1:1 + 2 * couples:2].set(giver - passed).at[2:2 + 2 * couples:2].set(sink + passed)
    return tallies[jax.random.permutation(jax.random.fold_in(rng, 2), count)]


def gaussian(rng, shape, scale, bound, cuts=(), held_as=jnp.bfloat16):
    entries = jax.random.normal(rng, shape, jnp.float32) * scale
    if len(cuts) > 0:
        entries = shard_levels(rng, shape, cuts, -0.22, 0.18) * entries
    return jnp.clip(entries, min=-bound, max=bound).astype(held_as)


def setup_inputs(seed: int = 0) -> dict:
    keys = jax.random.split(jax.random.key(seed), 18)
    return {
        "tokens": gaussian(keys[0], (SEQ_ALL, SEQ_LEN, D), 1.0, 6.0, ((0, 2), (1, 16))),
        "first_values": gaussian(keys[1], (SEQ_ALL, SEQ_LEN, D - VW), 1.0, 6.0, ((0, 2), (1, 16))),
        "teacher": draw_teacher(jax.random.fold_in(keys[17], 71), 0),
        "segment_ids": jax.vmap(lambda own: jnp.searchsorted(jnp.cumsum(ragged(own, SEGS, SEQ_LEN, DOC_MAX, 0)), jnp.arange(SEQ_LEN), side="right"))(jax.random.split(keys[3], SEQ_ALL)).reshape((SEQ_ALL, SEQ_LEN)).astype(jnp.int32),
        "lengths": draw_lengths(jax.random.fold_in(keys[17], 71), 0),
        "ln1_gain": jnp.clip(1.0 + 0.1 * jax.random.normal(keys[5], (D,), jnp.float32), 0.5, 1.5).astype(jnp.bfloat16),
        "ln1_bias": gaussian(keys[6], (D,), 0.2, 1.0, ((0, 2),)),
        "w_qkv": gaussian(keys[7], (D, 2 * D + VW), D ** -0.5, 0.21875, ((0, 2),)),
        "qv_bias": gaussian(keys[8], (D + VW,), 0.2, 1.0, ((0, 2),)),
        "w_out": gaussian(keys[9], (D, D), (D // HEAD) ** -0.5, 1.75, ((0, 2),)),
        "b_out": gaussian(keys[10], (D,), 0.2, 1.0, ((0, 2),)),
        "ln2_gain": jnp.clip(1.0 + 0.1 * jax.random.normal(keys[11], (D,), jnp.float32), 0.5, 1.5).astype(jnp.bfloat16),
        "ln2_bias": gaussian(keys[12], (D,), 0.2, 1.0, ((0, 2),)),
        "w_fc": gaussian(keys[13], (D, FF), D ** -0.5, 0.21875, ((0, 2),)),
        "b_fc": gaussian(keys[14], (FF,), 0.2, 1.0, ((0, 2),)),
        "w_proj": gaussian(keys[15], (FF, D), FF ** -0.5, 0.109375, ((0, 2),)),
        "b_proj": gaussian(keys[16], (D,), 0.2, 1.0, ((0, 2),)),
    }


@jax.custom_vjp
def low(v):
    return lax.optimization_barrier(v.astype(jnp.bfloat16)).astype(jnp.float32)

@jax.custom_vjp
def low_back(v):
    return v

def low_keep(v):
    return (low(v), None)

def low_pass(kept, grad):
    return (grad,)

def back_keep(v):
    return (v, None)

def back_low(kept, grad):
    return (low(grad),)
low.defvjp(low_keep, low_pass)
low_back.defvjp(back_keep, back_low)
EPS = 1e-05
NEG = -1e+30
HIGH = lax.Precision.HIGHEST

def matmul(left_side, right_side):
    return jnp.dot(left_side, right_side, precision=HIGH, preferred_element_type=jnp.float32)

def norm_layer(values, gain_vec, offset):
    average = lax.optimization_barrier(jnp.mean(values, axis=-1, keepdims=True))
    centred = values - average
    variance = lax.optimization_barrier(jnp.mean(centred * centred, axis=-1, keepdims=True))
    return centred * lax.rsqrt(variance + EPS) * gain_vec + offset

def sequence_forward(params, inputs, first, segs, length):
    norm1_gain, norm1_shift, qkv_weight, qv_shift, out_weight, out_shift, norm2_gain, norm2_shift, fc_weight, fc_shift, proj_weight, proj_shift = params
    normed1 = low(norm_layer(inputs, norm1_gain, norm1_shift))
    projected = matmul(normed1, qkv_weight)
    query_rows = low(low_back(projected[:, :D] + qv_shift[:D]))
    key_rows = low(low_back(projected[:, D:2 * D]))
    fresh_rows = low(low_back(projected[:, 2 * D:] + qv_shift[D:]))
    value_rows = jnp.concatenate([fresh_rows, first], axis=1)
    block_rows = min(512, SEQ_LEN)
    window = DOC_MAX + block_rows
    key_pad = jnp.concatenate([jnp.zeros((DOC_MAX, D), jnp.float32), key_rows], axis=0)
    value_pad = jnp.concatenate([jnp.zeros((DOC_MAX, D), jnp.float32), value_rows], axis=0)
    seg_pad = jnp.concatenate([jnp.full((DOC_MAX,), -1, jnp.int32), segs.astype(jnp.int32)])

    def one_block(first_row):
        query_part = lax.dynamic_slice_in_dim(query_rows, first_row, block_rows, 0).reshape(block_rows, HEADS, HEAD)
        key_part = lax.dynamic_slice_in_dim(key_pad, first_row, window, 0).reshape(window, HEADS, HEAD)
        value_part = lax.dynamic_slice_in_dim(value_pad, first_row, window, 0).reshape(window, HEADS, HEAD)
        seg_query = lax.dynamic_slice_in_dim(segs.astype(jnp.int32), first_row, block_rows, 0)
        seg_key = lax.dynamic_slice_in_dim(seg_pad, first_row, window, 0)
        query_pos = first_row + jnp.arange(block_rows, dtype=jnp.int32)
        key_pos = first_row - DOC_MAX + jnp.arange(window, dtype=jnp.int32)
        allowed = (seg_query[:, None] == seg_key[None, :]) & (key_pos[None, :] <= query_pos[:, None]) & ((key_pos[None, :] < length) | (key_pos[None, :] == query_pos[:, None]))
        scores = jnp.einsum('qhd,khd->hqk', query_part, key_part, precision=HIGH) * HEAD ** (-0.5)
        scores = jnp.where(allowed[None], low_back(scores), NEG)
        row_top = lax.optimization_barrier(jnp.max(scores, axis=-1, keepdims=True))
        log_total = row_top + jnp.log(lax.optimization_barrier(jnp.sum(jnp.exp(scores - row_top), axis=-1, keepdims=True)))
        probs = low(jnp.exp(scores - log_total) * allowed[None])
        return jnp.einsum('hqk,khd->qhd', probs, value_part, precision=HIGH).reshape(block_rows, D)
    starts = jnp.arange(SEQ_LEN // block_rows, dtype=jnp.int32) * block_rows
    attended = lax.map(jax.checkpoint(one_block), starts).reshape(SEQ_LEN, D)
    attended = low(low_back(attended))
    branch = low_back(matmul(attended, out_weight) + out_shift)
    resid = inputs + branch
    normed2 = low(norm_layer(resid, norm2_gain, norm2_shift))
    pre_act = low_back(matmul(normed2, fc_weight) + fc_shift)
    activ = low(jax.nn.gelu(pre_act, approximate=True))
    mixed = low_back(matmul(activ, proj_weight) + proj_shift)
    return resid + mixed

def layer_forward(inputs, first, params, segment_ids, lengths):

    def per_sequence(members):
        return sequence_forward(params, members[0], members[1], members[2], members[3])
    return lax.map(jax.checkpoint(per_sequence), (inputs, first, segment_ids, lengths))

def reference(tokens, first_values, teacher, segment_ids, lengths, ln1_gain, ln1_bias, w_qkv, qv_bias, w_out, b_out, ln2_gain, ln2_bias, w_fc, b_fc, w_proj, b_proj):
    params = tuple((member.astype(jnp.float32) for member in (ln1_gain, ln1_bias, w_qkv, qv_bias, w_out, b_out, ln2_gain, ln2_bias, w_fc, b_fc, w_proj, b_proj)))

    def model(inputs, first, weights):
        return layer_forward(inputs, first, weights, segment_ids, lengths)
    output, pullback = jax.vjp(model, tokens.astype(jnp.float32), first_values.astype(jnp.float32), params)
    positions = jnp.arange(SEQ_LEN, dtype=jnp.int32)
    valid_rows = (positions[None, :] < lengths[:, None]).astype(jnp.float32)
    deviation = (output - teacher.astype(jnp.float32)) * valid_rows[:, :, None]
    loss = jnp.sum(deviation * deviation) / (jnp.sum(valid_rows) * D)
    grad_tokens, grad_first, grads = pullback(deviation)
    return (loss, output.astype(jnp.bfloat16), grad_tokens, grad_first, grads[0], grads[1], grads[2], grads[3], grads[4], grads[5], grads[6], grads[7], grads[8], grads[9], grads[10], grads[11])
```

```python
import functools

import jax
import jax.numpy as jnp
from jax import lax
from jax.experimental import pallas as pl
from jax.experimental.pallas import tpu as pltpu
from jax.sharding import PartitionSpec as P

D = 768
HEADS = 12
HEAD = 64
DOC_MAX = 2048
VW = 384

EPS = 1e-05
NEG = -1e30

CHIPS = 8
GROUP = 2 * CHIPS
SEQS = 2
PER_SEQ = CHIPS // SEQS
UNITS = SEQS * HEADS // CHIPS
R = UNITS * HEAD
MESH = pl.DeviceIdType.MESH
DMA = pltpu.SemaphoreType.DMA


def norm_layer(values, gain_vec, offset):
    average = jnp.mean(values, axis=-1, keepdims=True)
    centred = values - average
    variance = jnp.mean(centred * centred, axis=-1, keepdims=True)
    return centred * lax.rsqrt(variance + EPS) * gain_vec + offset


def smooth_gate(values):
    return jax.nn.gelu(values, approximate=True)


def where_am_i():
    index, wsh = lax.axis_index("ctx"), lax.axis_index("wsh")
    base = index // GROUP * GROUP
    chip, core = index % GROUP // 2, index % 2

    def same_core(other):
        return (base + 2 * other + core, wsh)

    return chip, core, same_core, (base + 2 * chip + 1 - core, wsh)


def greet(peers):
    barrier = pltpu.get_barrier_semaphore()
    for peer in peers:
        pl.semaphore_signal(barrier, inc=1, device_id=peer, device_id_type=MESH)
    pl.semaphore_wait(barrier, len(peers))


def remote(src, dst, send, recv, peer):
    return pltpu.make_async_remote_copy(
        src_ref=src, dst_ref=dst, send_sem=send, recv_sem=recv, device_id=peer, device_id_type=MESH
    )


def lanes_of(chip, width):
    return pl.ds(pl.multiple_of(chip // PER_SEQ * width, width), width)


def rows_of(chip, first):
    return pl.ds(pl.multiple_of(first + chip % PER_SEQ * R, R), R)


def scatter_kernel(src, q_all, kv_all, send, recv, fsend, frecv, own):
    chip, core, same_core, sibling = where_am_i()
    width = q_all.shape[2]
    greet([same_core((chip + i) % CHIPS) for i in range(1, CHIPS)] + [sibling])
    block = 2 * chip + core

    def pieces(target):
        lanes = lanes_of(target, width)
        return (
            (src.at[rows_of(target, D), lanes], kv_all.at[block, pl.ds(0, R)]),
            (src.at[rows_of(target, 2 * D), lanes], kv_all.at[block, pl.ds(R, R)]),
            (src.at[rows_of(target, 0), lanes], q_all.at[chip]),
        )

    copies = []
    for i in range(1, CHIPS):
        target = (chip + i) % CHIPS
        copies.append(
            [
                remote(a, b, send.at[n, i], recv.at[n, i], same_core(target))
                for n, (a, b) in enumerate(pieces(target))
            ]
        )
        for copy in copies[-1]:
            copy.start()
    local = [pltpu.make_async_copy(a, b, own.at[n]) for n, (a, b) in enumerate(pieces(chip))]
    for copy in local:
        copy.start()
    for copy in local:
        copy.wait()
    forwards = []
    for i in range(CHIPS):
        if i:
            copies[i - 1][0].wait_recv()
            copies[i - 1][1].wait_recv()
        came = 2 * ((chip + CHIPS - i) % CHIPS) + core
        forwards.append(remote(kv_all.at[came], kv_all.at[came], fsend.at[i], frecv.at[i], sibling))
        forwards[-1].start()
    for i in range(1, CHIPS):
        copies[i - 1][2].wait_recv()
    for batch in copies:
        for copy in batch:
            copy.wait_send()
    for copy in forwards:
        copy.wait()


def home_kernel(src, dst, send, recv, own):
    chip, core, same_core, sibling = where_am_i()
    width = src.shape[2]
    greet([same_core((chip + i) % CHIPS) for i in range(1, CHIPS)])
    place = dst.at[rows_of(chip, 0), lanes_of(chip, width)]
    copies = []
    for i in range(1, CHIPS):
        target = (chip + i) % CHIPS
        copies.append(remote(src.at[target], place, send.at[i], recv.at[i], same_core(target)))
        copies[-1].start()
    local = pltpu.make_async_copy(src.at[chip], place, own)
    local.start()
    local.wait()
    for copy in copies:
        copy.wait()


def away_kernel(src, dst, send, recv, own):
    chip, core, same_core, sibling = where_am_i()
    width = dst.shape[2]
    greet([same_core((chip + i) % CHIPS) for i in range(1, CHIPS)])
    copies = []
    for i in range(1, CHIPS):
        target = (chip + i) % CHIPS
        piece = src.at[rows_of(target, 0), lanes_of(target, width)]
        copies.append(remote(piece, dst.at[chip], send.at[i], recv.at[i], same_core(target)))
        copies[-1].start()
    local = pltpu.make_async_copy(
        src.at[rows_of(chip, 0), lanes_of(chip, width)], dst.at[chip], own
    )
    local.start()
    local.wait()
    for copy in copies:
        copy.wait()


def return_kernel(dq, dkv, dst, give, take, final, send, recv, fsend, frecv, own):
    chip, core, same_core, sibling = where_am_i()
    width = dq.shape[2]
    greet([same_core((chip + i) % CHIPS) for i in range(1, CHIPS)] + [sibling])
    lanes = lanes_of(chip, width)
    halves = []
    for i in range(CHIPS):
        target = (chip + i) % CHIPS
        give[target] = dkv[2 * target + 1 - core].astype(jnp.bfloat16)
        halves.append(
            remote(give.at[target], take.at[target], fsend.at[i], frecv.at[i], sibling)
        )
        halves[-1].start()
    copies = []
    for i in range(1, CHIPS):
        target = (chip + i) % CHIPS
        copies.append(
            remote(
                dq.at[target],
                dst.at[rows_of(chip, 0), lanes],
                send.at[0, i],
                recv.at[0, i],
                same_core(target),
            )
        )
        copies[-1].start()
    local = [pltpu.make_async_copy(dq.at[chip], dst.at[rows_of(chip, 0), lanes], own.at[0])]
    local[0].start()
    for i in list(range(1, CHIPS)) + [0]:
        target = (chip + i) % CHIPS
        halves[i].wait_recv()
        final[target] = (dkv[2 * target + core] + take[target].astype(jnp.float32)).astype(
            jnp.bfloat16
        )
        for n in (1, 2):
            piece = final.at[target, pl.ds((n - 1) * R, R)]
            place = dst.at[rows_of(chip, n * D), lanes]
            if i:
                copies.append(
                    remote(piece, place, send.at[n, i], recv.at[n, i], same_core(target))
                )
                copies[-1].start()
            else:
                local.append(pltpu.make_async_copy(piece, place, own.at[n]))
                local[-1].start()
    for copy in local:
        copy.wait()
    for copy in halves:
        copy.wait_send()
    for copy in copies:
        copy.wait()


ANY = pl.BlockSpec(memory_space=pl.ANY)
VMEM = pl.BlockSpec(memory_space=pltpu.VMEM)
SMEM = pl.BlockSpec(memory_space=pltpu.SMEM)


def comm_params(number):
    return pltpu.CompilerParams(
        collective_id=number, has_side_effects=True, vmem_limit_bytes=48 << 20
    )


def scatter_heads(src, width):
    return pl.pallas_call(
        scatter_kernel,
        name="scatter_heads",
        out_shape=(
            jax.ShapeDtypeStruct((CHIPS, R, width), jnp.bfloat16),
            jax.ShapeDtypeStruct((GROUP, 2 * R, width), jnp.bfloat16),
        ),
        in_specs=[ANY],
        out_specs=(ANY, ANY),
        scratch_shapes=[
            DMA((3, CHIPS)),
            DMA((3, CHIPS)),
            DMA((CHIPS,)),
            DMA((CHIPS,)),
            DMA((3,)),
        ],
        compiler_params=comm_params(0),
    )(src)


def send_home(src):
    width = src.shape[2]
    return pl.pallas_call(
        home_kernel,
        name="send_home",
        out_shape=jax.ShapeDtypeStruct((D, SEQS * width), jnp.bfloat16),
        in_specs=[ANY],
        out_specs=ANY,
        scratch_shapes=[DMA((CHIPS,)), DMA((CHIPS,)), DMA],
        compiler_params=comm_params(1),
    )(src)


def send_away(src, width):
    return pl.pallas_call(
        away_kernel,
        name="send_away",
        out_shape=jax.ShapeDtypeStruct((CHIPS, R, width), jnp.bfloat16),
        in_specs=[ANY],
        out_specs=ANY,
        scratch_shapes=[DMA((CHIPS,)), DMA((CHIPS,)), DMA],
        compiler_params=comm_params(2),
    )(src)


def return_heads(dq, dkv):
    width = dq.shape[2]
    pair = pltpu.VMEM((CHIPS, 2 * R, width), jnp.bfloat16)
    return pl.pallas_call(
        return_kernel,
        name="return_heads",
        out_shape=jax.ShapeDtypeStruct((3 * D, SEQS * width), jnp.bfloat16),
        in_specs=[ANY, VMEM],
        out_specs=ANY,
        scratch_shapes=[
            pair,
            pair,
            pair,
            DMA((3, CHIPS)),
            DMA((3, CHIPS)),
            DMA((CHIPS,)),
            DMA((CHIPS,)),
            DMA((3,)),
        ],
        compiler_params=comm_params(3),
    )(dq, dkv)


def over_rows(left, right):
    return lax.dot_general(
        left, right, (((0,), (0,)), ((), ())), preferred_element_type=jnp.float32
    )


def over_lanes(left, right):
    return lax.dot_general(
        left, right, (((1,), (1,)), ((), ())), preferred_element_type=jnp.float32
    )


def head_rows(h, first=0):
    return slice(first + h * HEAD, first + (h + 1) * HEAD)


def forward_kernel(halo, info, q, kv, lo, out_wide, out_low, logs, top, total, accum):
    width = q.shape[2]
    core, length = info[CHIPS], info[CHIPS + 1]
    rows = lax.broadcasted_iota(jnp.int32, (width, width), 0)
    columns = lax.broadcasted_iota(jnp.int32, (1, width), 1)

    def one_query_block(j, unused):
        own = halo + 2 * j + core
        position = own * width + columns
        first = lo[j, 0:1, :]
        last = jnp.minimum(position, length - 1)

        diag = rows + own * width
        allowed = ((diag >= first) & (diag <= last)) | (diag == position)
        for h in range(UNITS):
            scores = over_rows(kv[own, head_rows(h), :], q[j, head_rows(h), :])
            scores = jnp.where(allowed, scores, NEG)
            peak = jnp.max(scores, axis=0, keepdims=True)
            expo = jnp.exp(scores - peak)
            top[h : h + 1, :] = peak
            total[h : h + 1, :] = jnp.sum(expo, axis=0, keepdims=True)
            accum[head_rows(h), :] = jnp.dot(
                kv[own, head_rows(h, R), :],
                expo.astype(jnp.bfloat16),
                preferred_element_type=jnp.float32,
            )

        def one_key_block(kb, unused):
            at = rows + kb * width
            allowed = (at >= first) & (at <= last)
            for h in range(UNITS):
                scores = over_rows(kv[kb, head_rows(h), :], q[j, head_rows(h), :])
                scores = jnp.where(allowed, scores, NEG)
                before = top[h : h + 1, :]
                peak = jnp.maximum(before, jnp.max(scores, axis=0, keepdims=True))
                expo = jnp.exp(scores - peak)
                shrink = jnp.exp(before - peak)
                top[h : h + 1, :] = peak
                total[h : h + 1, :] = total[h : h + 1, :] * shrink + jnp.sum(
                    expo, axis=0, keepdims=True
                )
                accum[head_rows(h), :] = accum[head_rows(h), :] * shrink + jnp.dot(
                    kv[kb, head_rows(h, R), :],
                    expo.astype(jnp.bfloat16),
                    preferred_element_type=jnp.float32,
                )
            return unused

        stop = jnp.minimum(own, (length + width - 1) // width)
        lax.fori_loop(info[j], stop, one_key_block, 0)
        for h in range(UNITS):
            result = accum[head_rows(h), :] / total[h : h + 1, :]
            out_wide[j, head_rows(h), :] = result
            out_low[j, head_rows(h), :] = result.astype(jnp.bfloat16)
            logs[j, h : h + 1, :] = top[h : h + 1, :] + jnp.log(total[h : h + 1, :])
        return unused

    lax.fori_loop(0, CHIPS, one_query_block, 0)


def attention_forward(info, q, kv, lo, halo):
    width = q.shape[2]
    return pl.pallas_call(
        functools.partial(forward_kernel, halo),
        name="attention_forward",
        out_shape=(
            jax.ShapeDtypeStruct((CHIPS, R, width), jnp.float32),
            jax.ShapeDtypeStruct((CHIPS, R, width), jnp.bfloat16),
            jax.ShapeDtypeStruct((CHIPS, 8, width), jnp.float32),
        ),
        in_specs=[SMEM, VMEM, VMEM, VMEM],
        out_specs=(VMEM, VMEM, VMEM),
        scratch_shapes=[
            pltpu.VMEM((8, width), jnp.float32),
            pltpu.VMEM((8, width), jnp.float32),
            pltpu.VMEM((R, width), jnp.float32),
        ],
        compiler_params=pltpu.CompilerParams(vmem_limit_bytes=48 << 20),
    )(info, q, kv, lo)


def backward_kernel(halo, info, q, kv, lo, grad, wide, logs, dq, dkv, query_acc, deltas):
    width = q.shape[2]
    core, length = info[CHIPS], info[CHIPS + 1]
    rows = lax.broadcasted_iota(jnp.int32, (width, width), 0)
    columns = lax.broadcasted_iota(jnp.int32, (1, width), 1)
    dkv[...] = jnp.zeros_like(dkv)

    def one_query_block(j, unused):
        own = halo + 2 * j + core
        position = own * width + columns
        first = lo[j, 0:1, :]
        last = jnp.minimum(position, length - 1)
        for h in range(UNITS):
            deltas[h : h + 1, :] = jnp.sum(
                grad[j, head_rows(h), :].astype(jnp.float32) * wide[j, head_rows(h), :],
                axis=0,
                keepdims=True,
            )
        query_acc[...] = jnp.zeros_like(query_acc)

        def block(kb, allowed):
            for h in range(UNITS):
                key, value = kv[kb, head_rows(h), :], kv[kb, head_rows(h, R), :]
                query, wanted = q[j, head_rows(h), :], grad[j, head_rows(h), :]
                scores = over_rows(key, query)
                probs = jnp.where(allowed, jnp.exp(scores - logs[j, h : h + 1, :]), 0.0)
                grad_probs = over_rows(value, wanted)
                grad_scores = (probs * (grad_probs - deltas[h : h + 1, :])).astype(jnp.bfloat16)
                dkv[kb, head_rows(h, R), :] += over_lanes(wanted, probs.astype(jnp.bfloat16))
                dkv[kb, head_rows(h), :] += over_lanes(query, grad_scores)
                query_acc[head_rows(h), :] += jnp.dot(
                    key, grad_scores, preferred_element_type=jnp.float32
                )

        diag = rows + own * width
        block(own, ((diag >= first) & (diag <= last)) | (diag == position))

        def one_key_block(kb, unused):
            at = rows + kb * width
            block(kb, (at >= first) & (at <= last))
            return unused

        stop = jnp.minimum(own, (length + width - 1) // width)
        lax.fori_loop(info[j], stop, one_key_block, 0)
        dq[j] = (query_acc[...] * HEAD ** (-0.5)).astype(jnp.bfloat16)
        return unused

    lax.fori_loop(0, CHIPS, one_query_block, 0)


def attention_backward(info, q, kv, lo, grad, wide, logs, halo):
    width = q.shape[2]
    return pl.pallas_call(
        functools.partial(backward_kernel, halo),
        name="attention_backward",
        out_shape=(
            jax.ShapeDtypeStruct((CHIPS, R, width), jnp.bfloat16),
            jax.ShapeDtypeStruct((halo + GROUP, 2 * R, width), jnp.float32),
        ),
        in_specs=[SMEM] + [VMEM] * 6,
        out_specs=(VMEM, VMEM),
        scratch_shapes=[
            pltpu.VMEM((R, width), jnp.float32),
            pltpu.VMEM((8, width), jnp.float32),
        ],
        compiler_params=pltpu.CompilerParams(vmem_limit_bytes=56 << 20),
    )(info, q, kv, lo, grad, wide, logs)


def local(
    tokens,
    first_values,
    teacher,
    segment_ids,
    lengths,
    ln1_gain,
    ln1_bias,
    w_qkv,
    qv_bias,
    w_out,
    b_out,
    ln2_gain,
    ln2_bias,
    w_fc,
    b_fc,
    w_proj,
    b_proj,
):
    seq_count, width = tokens.shape[0], tokens.shape[1]
    row_count = seq_count * width
    ctx_size = lax.axis_size("ctx")
    ctx_index = lax.axis_index("ctx")
    groups = ctx_size // GROUP
    halo = pl.cdiv(DOC_MAX - 1, width) if groups > 1 else 0
    assert seq_count == SEQS and ctx_size % GROUP == 0 and halo <= GROUP
    chip, core = ctx_index % GROUP // 2, ctx_index % 2
    (
        norm1_gain,
        norm1_shift,
        qkv_weight,
        qv_shift,
        out_weight,
        out_shift,
        norm2_gain,
        norm2_shift,
        fc_weight,
        fc_shift,
        proj_weight,
        proj_shift,
    ) = (
        lax.all_gather(part, "wsh", axis=0, tiled=True)
        for part in (
            ln1_gain,
            ln1_bias,
            w_qkv,
            qv_bias,
            w_out,
            b_out,
            ln2_gain,
            ln2_bias,
            w_fc,
            b_fc,
            w_proj,
            b_proj,
        )
    )
    query_pos = ctx_index * width + jnp.arange(width, dtype=jnp.int32)

    window = (halo + GROUP) * width
    start = ctx_index // GROUP * GROUP * width - halo * width
    ids = lax.dynamic_index_in_dim(segment_ids, chip // PER_SEQ, 0, keepdims=False)
    if halo:
        ids = jnp.concatenate([jnp.full((halo * width,), -1, jnp.int32), ids])
    ids = lax.dynamic_slice_in_dim(ids, start + halo * width, window, 0)
    mine = lax.dynamic_index_in_dim(
        ids[halo * width :].reshape(CHIPS, 2, width), core, 1, keepdims=False
    )
    lo = jnp.sum((ids[None, None, :] < mine[:, :, None]).astype(jnp.int32), axis=-1)
    length = lax.dynamic_index_in_dim(lengths, chip // PER_SEQ, 0, keepdims=False) - start
    info = jnp.concatenate([lo[:, 0] // width, jnp.stack([core, length])]).astype(jnp.int32)
    lo = jnp.broadcast_to(lo[:, None, :], (CHIPS, 8, width))

    inputs = tokens.reshape(row_count, D).astype(jnp.float32)
    normed1, norm1_back = jax.vjp(
        norm_layer, inputs, norm1_gain.astype(jnp.float32), norm1_shift.astype(jnp.float32)
    )
    normed1_low = normed1.astype(jnp.bfloat16)
    projected = lax.dot_general(
        qkv_weight, normed1_low, (((0,), (1,)), ((), ())), preferred_element_type=jnp.float32
    )
    shift_wide = qv_shift.astype(jnp.float32)[:, None]
    sent = jnp.concatenate(
        [
            (projected[:D] + shift_wide[:D]).astype(jnp.bfloat16) * HEAD ** (-0.5),
            projected[D : 2 * D].astype(jnp.bfloat16),
            (projected[2 * D :] + shift_wide[D:]).astype(jnp.bfloat16),
            first_values.reshape(row_count, D - VW).T,
        ],
        axis=0,
    )
    q_all, kv_all = scatter_heads(sent, width)
    if halo:
        ahead = [(i, i + GROUP) for i in range(ctx_size - GROUP)]
        kv_all = jnp.concatenate(
            [lax.ppermute(kv_all[GROUP - halo :], "ctx", ahead), kv_all], axis=0
        )
    out_wide, out_low, logs = attention_forward(info, q_all, kv_all, lo, halo)
    attended = send_home(out_low)
    resid = inputs + over_rows(attended, out_weight) + out_shift.astype(jnp.float32)
    normed2, norm2_back = jax.vjp(
        norm_layer, resid, norm2_gain.astype(jnp.float32), norm2_shift.astype(jnp.float32)
    )
    normed2_low = normed2.astype(jnp.bfloat16)
    pre_act = jnp.dot(normed2_low, fc_weight, preferred_element_type=jnp.float32) + fc_shift.astype(
        jnp.float32
    )
    activ, gelu_back = jax.vjp(smooth_gate, pre_act)
    activ_low = activ.astype(jnp.bfloat16)
    result = (
        resid
        + jnp.dot(activ_low, proj_weight, preferred_element_type=jnp.float32)
        + proj_shift.astype(jnp.float32)
    )
    valid_rows = (query_pos[None, :] < lengths[:, None]).astype(jnp.float32)
    deviation = (
        result.reshape(seq_count, width, D) - teacher.astype(jnp.float32)
    ) * valid_rows[:, :, None]
    squares, valid_count = lax.psum(
        (jnp.sum(deviation * deviation), jnp.sum(valid_rows)), ("ctx", "wsh")
    )
    loss = squares / (valid_count * D)
    grad_output = deviation.reshape(row_count, D)
    grad_mixed = grad_output.astype(jnp.bfloat16)
    grad_proj_w = over_rows(activ_low, grad_mixed)
    grad_proj_b = jnp.sum(grad_mixed.astype(jnp.float32), axis=0)
    grad_activ = over_lanes(grad_mixed, proj_weight)
    grad_pre = gelu_back(grad_activ)[0].astype(jnp.bfloat16)
    grad_fc_w = over_rows(normed2_low, grad_pre)
    grad_fc_b = jnp.sum(grad_pre.astype(jnp.float32), axis=0)
    grad_normed2 = over_lanes(grad_pre, fc_weight)
    grad_resid_norm, grad_g2, grad_b2 = norm2_back(grad_normed2)
    grad_resid = grad_output + grad_resid_norm
    grad_branch = grad_resid.astype(jnp.bfloat16)
    grad_out_w = jnp.dot(attended, grad_branch, preferred_element_type=jnp.float32)
    grad_out_b = jnp.sum(grad_branch.astype(jnp.float32), axis=0)
    grad_attended = over_lanes(out_weight, grad_branch).astype(jnp.bfloat16)
    grad_all = send_away(grad_attended, width)
    dq, dkv = attention_backward(info, q_all, kv_all, lo, grad_all, out_wide, logs, halo)
    if halo:
        behind = [(i + GROUP, i) for i in range(ctx_size - GROUP)]
        over = lax.ppermute(dkv[:halo].astype(jnp.bfloat16), "ctx", behind)
        dkv = dkv[halo:].at[GROUP - halo :].add(over.astype(jnp.float32))
    grads_t = return_heads(dq, dkv)
    grad_projected = grads_t[: 2 * D + VW]
    grad_first = grads_t[2 * D + VW :].T.astype(jnp.float32)
    grad_qkv_w = lax.dot_general(
        normed1_low, grad_projected, (((0,), (1,)), ((), ())), preferred_element_type=jnp.float32
    )
    grad_sums = jnp.sum(grad_projected.astype(jnp.float32), axis=1)
    grad_qv_b = jnp.concatenate([grad_sums[:D], grad_sums[2 * D :]])
    grad_normed1 = lax.dot_general(
        grad_projected, qkv_weight, (((0,), (1,)), ((), ())), preferred_element_type=jnp.float32
    )
    grad_input_norm, grad_g1, grad_b1 = norm1_back(grad_normed1)
    grad_inputs = grad_resid + grad_input_norm
    grads = (
        grad_g1,
        grad_b1,
        grad_qkv_w,
        grad_qv_b,
        grad_out_w,
        grad_out_b,
        grad_g2,
        grad_b2,
        grad_fc_w,
        grad_fc_b,
        grad_proj_w,
        grad_proj_b,
    )
    shares = tuple(
        lax.psum_scatter(
            part.astype(jnp.bfloat16), "wsh", scatter_dimension=0, tiled=True
        ).astype(jnp.float32)
        for part in grads
    )
    totals = tuple(lax.psum(shares, "ctx"))
    return (
        loss,
        result.reshape(seq_count, width, D).astype(jnp.bfloat16),
        grad_inputs.reshape(seq_count, width, D),
        grad_first.reshape(seq_count, width, D - VW),
    ) + totals


def solution(mesh):
    whole, rows, vector = P("wsh", "ctx", None), P("wsh", None), P("wsh")
    in_specs = (whole, whole, whole, rows, vector) + (
        vector,
        vector,
        rows,
        vector,
        rows,
        vector,
        vector,
        vector,
        rows,
        vector,
        rows,
        vector,
    )
    out_specs = (P(), whole, whole, whole) + in_specs[5:]
    return jax.shard_map(local, mesh=mesh, in_specs=in_specs, out_specs=out_specs, check_vma=False)
```

```python
import functools

import jax
import jax.numpy as jnp
from jax import lax
from jax.experimental import pallas as pl
from jax.experimental.pallas import tpu as pltpu
from jax.sharding import PartitionSpec as P

D = 768
HEADS = 12
HEAD = 64
DOC_MAX = 2048
VW = 384

EPS = 1e-05
NEG = -1e30

CHIPS = 8
GROUP = 2 * CHIPS
SEQS = 2
PER_SEQ = CHIPS // SEQS
UNITS = SEQS * HEADS // CHIPS
R = UNITS * HEAD
MESH = pl.DeviceIdType.MESH
DMA = pltpu.SemaphoreType.DMA


def norm_layer(values, gain_vec, offset):
    average = jnp.mean(values, axis=-1, keepdims=True)
    centred = values - average
    variance = jnp.mean(centred * centred, axis=-1, keepdims=True)
    return centred * lax.rsqrt(variance + EPS) * gain_vec + offset


def smooth_gate(values):
    return jax.nn.gelu(values, approximate=True)


def where_am_i():
    index, wsh = lax.axis_index("ctx"), lax.axis_index("wsh")
    base = index // GROUP * GROUP
    chip, core = index % GROUP // 2, index % 2

    def same_core(other):
        return (base + 2 * other + core, wsh)

    sibling, partner = (base + 2 * chip + 1 - core, wsh), (index, 1 - wsh)
    return chip, core, same_core, sibling, partner, wsh


def greet(peers):
    barrier = pltpu.get_barrier_semaphore()
    for peer in peers:
        pl.semaphore_signal(barrier, inc=1, device_id=peer, device_id_type=MESH)
    pl.semaphore_wait(barrier, len(peers))


def remote(src, dst, send, recv, peer):
    return pltpu.make_async_remote_copy(
        src_ref=src, dst_ref=dst, send_sem=send, recv_sem=recv, device_id=peer, device_id_type=MESH
    )


def lanes_of(chip, width):
    return pl.ds(pl.multiple_of(chip // PER_SEQ * width, width), width)


def rows_of(chip, first):
    return pl.ds(pl.multiple_of(first + chip % PER_SEQ * R, R), R)


def share_start(shard, full, sems, partner, core, wsh):
    xs, xr, fs, fr, own = sems
    sends = []
    for k in range(shard.shape[1]):
        sends.append(remote(shard.at[core, k], full.at[wsh, core, k], xs.at[k], xr.at[k], partner))
        sends[-1].start()
    local = pltpu.make_async_copy(shard, full.at[wsh], own)
    local.start()
    return sends, local


def share_pass(state, k, full, sems, sibling, core, wsh):
    xs, xr, fs, fr, own = sems
    state[0][k].wait_recv()
    piece = full.at[1 - wsh, core, k]
    forward = remote(piece, piece, fs.at[k], fr.at[k], sibling)
    forward.start()
    return forward


def share_end(state, forwards):
    state[1].wait()
    for copy in state[0]:
        copy.wait_send()
    for copy in forwards:
        copy.wait()


def share_scratch(shard):
    chunks = shard.shape[1]
    return [DMA((chunks,)), DMA((chunks,)), DMA((chunks,)), DMA((chunks,)), DMA]


def full_of(shard):
    return jax.ShapeDtypeStruct((2,) + shard.shape, shard.dtype)


def first_kernel(weight, small, full, all_small, *sems):
    chip, core, same_core, sibling, partner, wsh = where_am_i()
    greet([sibling, partner])
    pack = share_start(small, all_small, sems[5:], partner, core, wsh)
    state = share_start(weight, full, sems[:5], partner, core, wsh)
    passed = [share_pass(pack, 0, all_small, sems[5:], sibling, core, wsh)]
    forwards = [
        share_pass(state, k, full, sems[:5], sibling, core, wsh) for k in range(weight.shape[1])
    ]
    share_end(pack, passed)
    share_end(state, forwards)


def scatter_kernel(src, weight_a, weight_b, q_all, kv_all, full_a, full_b, *sems):
    chip, core, same_core, sibling, partner, wsh = where_am_i()
    send, recv, fsend, frecv, own = sems[:5]
    sems_a, sems_b = sems[5:10], sems[10:]
    width = q_all.shape[2]
    greet([same_core((chip + i) % CHIPS) for i in range(1, CHIPS)] + [sibling, partner])
    block = 2 * chip + core

    def pieces(target):
        lanes = lanes_of(target, width)
        return (
            (src.at[rows_of(target, D), lanes], kv_all.at[block, pl.ds(0, R)]),
            (src.at[rows_of(target, 2 * D), lanes], kv_all.at[block, pl.ds(R, R)]),
            (src.at[rows_of(target, 0), lanes], q_all.at[chip]),
        )

    copies = []
    for i in range(1, CHIPS):
        target = (chip + i) % CHIPS
        copies.append(
            [
                remote(a, b, send.at[n, i], recv.at[n, i], same_core(target))
                for n, (a, b) in enumerate(pieces(target))
            ]
        )
        for copy in copies[-1]:
            copy.start()
    local = [pltpu.make_async_copy(a, b, own.at[n]) for n, (a, b) in enumerate(pieces(chip))]
    for copy in local:
        copy.start()
    state_a = share_start(weight_a, full_a, sems_a, partner, core, wsh)
    state_b = share_start(weight_b, full_b, sems_b, partner, core, wsh)
    for copy in local:
        copy.wait()
    forwards = []
    for i in range(CHIPS):
        if i:
            copies[i - 1][0].wait_recv()
            copies[i - 1][1].wait_recv()
        came = 2 * ((chip + CHIPS - i) % CHIPS) + core
        forwards.append(remote(kv_all.at[came], kv_all.at[came], fsend.at[i], frecv.at[i], sibling))
        forwards[-1].start()
    passed_a = [
        share_pass(state_a, k, full_a, sems_a, sibling, core, wsh)
        for k in range(weight_a.shape[1])
    ]
    passed_b = [
        share_pass(state_b, k, full_b, sems_b, sibling, core, wsh)
        for k in range(weight_b.shape[1])
    ]
    for i in range(1, CHIPS):
        copies[i - 1][2].wait_recv()
    for batch in copies:
        for copy in batch:
            copy.wait_send()
    for copy in forwards:
        copy.wait()
    share_end(state_a, passed_a)
    share_end(state_b, passed_b)


def home_kernel(src, weight, dst, full, send, recv, own, *sems):
    chip, core, same_core, sibling, partner, wsh = where_am_i()
    width = src.shape[2]
    greet([same_core((chip + i) % CHIPS) for i in range(1, CHIPS)] + [sibling, partner])
    place = dst.at[rows_of(chip, 0), lanes_of(chip, width)]
    copies = []
    for i in range(1, CHIPS):
        target = (chip + i) % CHIPS
        copies.append(remote(src.at[target], place, send.at[i], recv.at[i], same_core(target)))
        copies[-1].start()
    state = share_start(weight, full, sems, partner, core, wsh)
    local = pltpu.make_async_copy(src.at[chip], place, own)
    local.start()
    passed = [
        share_pass(state, k, full, sems, sibling, core, wsh) for k in range(weight.shape[1])
    ]
    local.wait()
    for copy in copies:
        copy.wait()
    share_end(state, passed)


def add_into(dst, parts):
    rows = dst.shape[0]
    step = 16 if rows % 16 == 0 else 8

    def one(i, unused):
        at = pl.ds(pl.multiple_of(i * step, step), step)
        total = parts[0][at, :].astype(jnp.float32)
        for part in parts[1:]:
            total = total + part[at, :].astype(jnp.float32)
        dst[at, :] = total.astype(dst.dtype)
        return unused

    lax.fori_loop(0, rows // step, one, 0)


def pair_start(terms, buffers, sems, sibling, core, wsh):
    from_sibling, for_partner, from_partner = buffers
    ss, sr, xs, xr = sems
    gives = []
    for half in range(2):
        which = 1 - wsh if half == 0 else wsh
        for k in range(terms.shape[2]):
            gives.append(
                remote(
                    terms.at[which, 1 - core, k],
                    from_sibling.at[half, k],
                    ss.at[half, k],
                    sr.at[half, k],
                    sibling,
                )
            )
            gives[-1].start()
    return gives


def pair_cross(terms, buffers, sems, gives, partner, core, wsh):
    from_sibling, for_partner, from_partner = buffers
    ss, sr, xs, xr = sems
    sends = []
    for k in range(terms.shape[2]):
        gives[k].wait_recv()
        add_into(for_partner.at[k], [terms.at[1 - wsh, core, k], from_sibling.at[0, k]])
        sends.append(remote(for_partner.at[k], from_partner.at[k], xs.at[k], xr.at[k], partner))
        sends[-1].start()
    return sends


def pair_end(terms, buffers, gives, sends, result, core, wsh):
    from_sibling, for_partner, from_partner = buffers
    chunks = terms.shape[2]
    for k in range(chunks):
        gives[chunks + k].wait_recv()
        sends[k].wait_recv()
        add_into(
            result.at[k], [terms.at[wsh, core, k], from_sibling.at[1, k], from_partner.at[k]]
        )
    for copy in gives + sends:
        copy.wait_send()


def pair_scratch(terms):
    chunks, rows, columns = terms.shape[2:]
    return [
        pltpu.VMEM((2, chunks, rows, columns), jnp.bfloat16),
        pltpu.VMEM((chunks, rows, columns), jnp.bfloat16),
        pltpu.VMEM((chunks, rows, columns), jnp.bfloat16),
        DMA((2, chunks)),
        DMA((2, chunks)),
        DMA((chunks,)),
        DMA((chunks,)),
    ]


def away_kernel(src, terms, dst, result, send, recv, own, *pair):
    chip, core, same_core, sibling, partner, wsh = where_am_i()
    width = dst.shape[2]
    greet([same_core((chip + i) % CHIPS) for i in range(1, CHIPS)] + [sibling, partner])
    copies = []
    for i in range(1, CHIPS):
        target = (chip + i) % CHIPS
        piece = src.at[rows_of(target, 0), lanes_of(target, width)]
        copies.append(remote(piece, dst.at[chip], send.at[i], recv.at[i], same_core(target)))
        copies[-1].start()
    local = pltpu.make_async_copy(
        src.at[rows_of(chip, 0), lanes_of(chip, width)], dst.at[chip], own
    )
    local.start()
    gives = pair_start(terms, pair[:3], pair[3:], sibling, core, wsh)
    sends = pair_cross(terms, pair[:3], pair[3:], gives, partner, core, wsh)
    pair_end(terms, pair[:3], gives, sends, result, core, wsh)
    local.wait()
    for copy in copies:
        copy.wait()


def return_kernel(dq, dkv, terms_a, terms_b, dst, result_a, result_b, *scratch):
    chip, core, same_core, sibling, partner, wsh = where_am_i()
    give, take, final, send, recv, fsend, frecv, own = scratch[:8]
    pair_a, pair_b = scratch[8:15], scratch[15:]
    width = dq.shape[2]
    greet([same_core((chip + i) % CHIPS) for i in range(1, CHIPS)] + [sibling, partner])
    lanes = lanes_of(chip, width)
    halves = []
    for i in range(CHIPS):
        target = (chip + i) % CHIPS
        give[target] = dkv[2 * target + 1 - core].astype(jnp.bfloat16)
        halves.append(
            remote(give.at[target], take.at[target], fsend.at[i], frecv.at[i], sibling)
        )
        halves[-1].start()
    copies = []
    for i in range(1, CHIPS):
        target = (chip + i) % CHIPS
        copies.append(
            remote(
                dq.at[target],
                dst.at[rows_of(chip, 0), lanes],
                send.at[0, i],
                recv.at[0, i],
                same_core(target),
            )
        )
        copies[-1].start()
    local = [pltpu.make_async_copy(dq.at[chip], dst.at[rows_of(chip, 0), lanes], own.at[0])]
    local[0].start()
    gives_a = pair_start(terms_a, pair_a[:3], pair_a[3:], sibling, core, wsh)
    gives_b = pair_start(terms_b, pair_b[:3], pair_b[3:], sibling, core, wsh)
    for i in list(range(1, CHIPS)) + [0]:
        target = (chip + i) % CHIPS
        halves[i].wait_recv()
        final[target] = (dkv[2 * target + core] + take[target].astype(jnp.float32)).astype(
            jnp.bfloat16
        )
        for n in (1, 2):
            piece = final.at[target, pl.ds((n - 1) * R, R)]
            place = dst.at[rows_of(chip, n * D), lanes]
            if i:
                copies.append(
                    remote(piece, place, send.at[n, i], recv.at[n, i], same_core(target))
                )
                copies[-1].start()
            else:
                local.append(pltpu.make_async_copy(piece, place, own.at[n]))
                local[-1].start()
    sends_a = pair_cross(terms_a, pair_a[:3], pair_a[3:], gives_a, partner, core, wsh)
    sends_b = pair_cross(terms_b, pair_b[:3], pair_b[3:], gives_b, partner, core, wsh)
    pair_end(terms_a, pair_a[:3], gives_a, sends_a, result_a, core, wsh)
    pair_end(terms_b, pair_b[:3], gives_b, sends_b, result_b, core, wsh)
    for copy in local:
        copy.wait()
    for copy in halves:
        copy.wait_send()
    for copy in copies:
        copy.wait()


def finish_kernel(small, *refs):
    chip, core, same_core, sibling, partner, wsh = where_am_i()
    sums, terms = refs[:3], refs[3]
    all_small, outs = refs[4], refs[5:9]
    kept = refs[9]
    pair = refs[10:17]
    stages = [refs[17 + 11 * n : 28 + 11 * n] for n in range(4)]
    small_take, small_send, small_recv = refs[61:]
    a, b = chip // 2, chip % 2
    along_a = [(a + i) % 4 for i in range(4)]
    other_b = same_core(2 * a + 1 - b)
    peers_a = [same_core(2 * other + b) for other in along_a]
    greet([sibling, partner, other_b] + peers_a[1:])

    gives = pair_start(terms, pair[:3], pair[3:], sibling, core, wsh)
    mine = list(sums) + [kept]

    def start_b(n):
        took_b, added, took_a, bs, br, zs, zr, gs, gr, ks, kr = stages[n]
        copy = remote(mine[n].at[pl.ds(pl.multiple_of(4 - 4 * b, 4), 4)], took_b, bs, br, other_b)
        copy.start()
        return copy

    def start_a(n, swap):
        took_b, added, took_a, bs, br, zs, zr, gs, gr, ks, kr = stages[n]
        swap.wait_recv()
        copies = []
        for i in (1, 2, 3, 0):
            other = along_a[i]
            add_into(added.at[other], [mine[n].at[4 * b + other], took_b.at[other]])
            if i:
                copies.append(
                    remote(added.at[other], took_a.at[i - 1], zs.at[i], zr.at[i], peers_a[i])
                )
                copies[-1].start()
        return copies

    def give_out(n, copies):
        took_b, added, took_a, bs, br, zs, zr, gs, gr, ks, kr = stages[n]
        out = outs[n]
        for copy in copies:
            copy.wait_recv()
        piece = out.at[core, 4 * b + a]
        add_into(piece, [added.at[a], took_a.at[0], took_a.at[1], took_a.at[2]])
        news = []
        for i in (1, 2, 3):
            news.append(remote(piece, piece, gs.at[0, i], gr.at[0, i], peers_a[i]))
        news.append(remote(piece, piece, gs.at[1, 0], gr.at[1, 0], other_b))
        news.append(remote(piece, piece, ks.at[0, 0], kr.at[0, 0], sibling))
        for copy in news:
            copy.start()
        return news

    def hand_on(n, news):
        took_b, added, took_a, bs, br, zs, zr, gs, gr, ks, kr = stages[n]
        out = outs[n]
        more = []
        for i in (1, 2, 3):
            news[i - 1].wait_recv()
            piece = out.at[core, 4 * b + (a + 4 - i) % 4]
            more.append(remote(piece, piece, gs.at[1, i], gr.at[1, i], other_b))
            more.append(remote(piece, piece, ks.at[0, i], kr.at[0, i], sibling))
            for copy in more[-2:]:
                copy.start()
        return more

    def last_pass(n, news, more):
        took_b, added, took_a, bs, br, zs, zr, gs, gr, ks, kr = stages[n]
        out = outs[n]
        final = []
        for i in range(4):
            (news[3] if i == 0 else more[2 * i - 2]).wait_recv()
            piece = out.at[core, 4 - 4 * b + (a + 4 - i) % 4]
            final.append(remote(piece, piece, ks.at[1, i], kr.at[1, i], sibling))
            final[-1].start()
        return final

    swaps = [start_b(n) for n in range(3)]
    sends = pair_cross(terms, pair[:3], pair[3:], gives, partner, core, wsh)

    all_small[...] = small[...]
    order = [sibling, partner, other_b]
    for n, peer in enumerate(order):
        small_take[3 + n] = all_small[...]
        copy = remote(
            small_take.at[3 + n], small_take.at[n], small_send.at[n], small_recv.at[n], peer
        )
        copy.start()
        copy.wait()
        all_small[...] = all_small[...] + small_take[n]
    small_take[6 + a] = all_small[...]
    smalls = []
    for i in (1, 2, 3):
        smalls.append(
            remote(
                small_take.at[6 + a],
                small_take.at[6 + a],
                small_send.at[2 + i],
                small_recv.at[2 + i],
                peers_a[i],
            )
        )
        smalls[-1].start()

    crossings = [start_a(n, swaps[n]) for n in range(3)]
    pair_end(terms, pair[:3], gives, sends, kept, core, wsh)
    swaps.append(start_b(3))
    news = [give_out(n, crossings[n]) for n in range(3)]
    crossings.append(start_a(3, swaps[3]))
    more = [hand_on(n, news[n]) for n in range(3)]
    news.append(give_out(3, crossings[3]))
    final = [last_pass(n, news[n], more[n]) for n in range(3)]
    more.append(hand_on(3, news[3]))
    final.append(last_pass(3, news[3], more[3]))
    for copy in smalls:
        copy.wait()
    all_small[...] = small_take[6] + small_take[7] + small_take[8] + small_take[9]
    for n in range(4):
        swaps[n].wait_send()
        for copy in crossings[n] + news[n] + more[n] + final[n]:
            copy.wait_send()
        news[n][4].wait_recv()
        for i in (1, 2, 3):
            more[n][2 * i - 1].wait_recv()
        for copy in final[n]:
            copy.wait_recv()


ANY = pl.BlockSpec(memory_space=pl.ANY)
VMEM = pl.BlockSpec(memory_space=pltpu.VMEM)
SMEM = pl.BlockSpec(memory_space=pltpu.SMEM)


def comm_params(number, mib=48):
    return pltpu.CompilerParams(
        collective_id=number, has_side_effects=True, vmem_limit_bytes=mib << 20
    )


def gather_first(weight, small):
    return pl.pallas_call(
        first_kernel,
        name="gather_first",
        out_shape=(full_of(weight), full_of(small)),
        in_specs=[ANY, ANY],
        out_specs=(ANY, ANY),
        scratch_shapes=share_scratch(weight) + share_scratch(small),
        compiler_params=comm_params(4),
    )(weight, small)


def scatter_heads(src, weight_a, weight_b, width):
    return pl.pallas_call(
        scatter_kernel,
        name="scatter_heads",
        out_shape=(
            jax.ShapeDtypeStruct((CHIPS, R, width), jnp.bfloat16),
            jax.ShapeDtypeStruct((GROUP, 2 * R, width), jnp.bfloat16),
            full_of(weight_a),
            full_of(weight_b),
        ),
        in_specs=[ANY] * 3,
        out_specs=(ANY,) * 4,
        scratch_shapes=[
            DMA((3, CHIPS)),
            DMA((3, CHIPS)),
            DMA((CHIPS,)),
            DMA((CHIPS,)),
            DMA((3,)),
        ]
        + share_scratch(weight_a)
        + share_scratch(weight_b),
        compiler_params=comm_params(0),
    )(src, weight_a, weight_b)


def send_home(src, weight):
    width = src.shape[2]
    return pl.pallas_call(
        home_kernel,
        name="send_home",
        out_shape=(jax.ShapeDtypeStruct((D, SEQS * width), jnp.bfloat16), full_of(weight)),
        in_specs=[ANY, ANY],
        out_specs=(ANY, ANY),
        scratch_shapes=[DMA((CHIPS,)), DMA((CHIPS,)), DMA] + share_scratch(weight),
        compiler_params=comm_params(1),
    )(src, weight)


def sum_of(terms):
    return jax.ShapeDtypeStruct(terms.shape[2:], jnp.bfloat16)


def send_away(src, terms, width):
    return pl.pallas_call(
        away_kernel,
        name="send_away",
        out_shape=(jax.ShapeDtypeStruct((CHIPS, R, width), jnp.bfloat16), sum_of(terms)),
        in_specs=[ANY, VMEM],
        out_specs=(ANY, VMEM),
        scratch_shapes=[DMA((CHIPS,)), DMA((CHIPS,)), DMA] + pair_scratch(terms),
        compiler_params=comm_params(2),
    )(src, terms)


def return_heads(dq, dkv, terms_a, terms_b):
    width = dq.shape[2]
    pair = pltpu.VMEM((CHIPS, 2 * R, width), jnp.bfloat16)
    return pl.pallas_call(
        return_kernel,
        name="return_heads",
        out_shape=(
            jax.ShapeDtypeStruct((3 * D, SEQS * width), jnp.bfloat16),
            sum_of(terms_a),
            sum_of(terms_b),
        ),
        in_specs=[ANY, VMEM, VMEM, VMEM],
        out_specs=(ANY, VMEM, VMEM),
        scratch_shapes=[
            pair,
            pair,
            pair,
            DMA((3, CHIPS)),
            DMA((3, CHIPS)),
            DMA((CHIPS,)),
            DMA((CHIPS,)),
            DMA((3,)),
        ]
        + pair_scratch(terms_a)
        + pair_scratch(terms_b),
        compiler_params=comm_params(3, 56),
    )(dq, dkv, terms_a, terms_b)


def finish_sums(small, sums, terms):
    def stage(total):
        rows, columns = total.shape[1:]
        four = pltpu.VMEM((4, rows, columns), jnp.bfloat16)
        return [
            four,
            four,
            pltpu.VMEM((3, rows, columns), jnp.bfloat16),
            DMA,
            DMA,
            DMA((4,)),
            DMA((4,)),
            DMA((2, 4)),
            DMA((2, 4)),
            DMA((2, 4)),
            DMA((2, 4)),
        ]

    kept = sum_of(terms)
    whole = [*sums, kept]
    return pl.pallas_call(
        finish_kernel,
        name="finish_sums",
        out_shape=[jax.ShapeDtypeStruct(small.shape, small.dtype)]
        + [jax.ShapeDtypeStruct((2,) + total.shape, total.dtype) for total in whole],
        in_specs=[VMEM] * 5,
        out_specs=[VMEM] * 5,
        scratch_shapes=[pltpu.VMEM(kept.shape, kept.dtype)]
        + pair_scratch(terms)
        + [item for total in whole for item in stage(total)]
        + [
            pltpu.VMEM((10,) + small.shape, small.dtype),
            DMA((6,)),
            DMA((6,)),
        ],
        compiler_params=comm_params(5, 56),
    )(small, *sums, terms)


def over_rows(left, right):
    return lax.dot_general(
        left, right, (((0,), (0,)), ((), ())), preferred_element_type=jnp.float32
    )


def over_lanes(left, right):
    return lax.dot_general(
        left, right, (((1,), (1,)), ((), ())), preferred_element_type=jnp.float32
    )


def head_rows(h, first=0):
    return slice(first + h * HEAD, first + (h + 1) * HEAD)


def forward_kernel(halo, info, q, kv, lo, out_wide, out_low, logs, top, total, accum):
    width = q.shape[2]
    core, length = info[CHIPS], info[CHIPS + 1]
    rows = lax.broadcasted_iota(jnp.int32, (width, width), 0)
    columns = lax.broadcasted_iota(jnp.int32, (1, width), 1)

    def one_query_block(j, unused):
        own = halo + 2 * j + core
        position = own * width + columns
        first = lo[j, 0:1, :]
        last = jnp.minimum(position, length - 1)

        diag = rows + own * width
        allowed = ((diag >= first) & (diag <= last)) | (diag == position)
        for h in range(UNITS):
            scores = over_rows(kv[own, head_rows(h), :], q[j, head_rows(h), :])
            scores = jnp.where(allowed, scores, NEG)
            peak = jnp.max(scores, axis=0, keepdims=True)
            expo = jnp.exp(scores - peak)
            top[h : h + 1, :] = peak
            total[h : h + 1, :] = jnp.sum(expo, axis=0, keepdims=True)
            accum[head_rows(h), :] = jnp.dot(
                kv[own, head_rows(h, R), :],
                expo.astype(jnp.bfloat16),
                preferred_element_type=jnp.float32,
            )

        def one_key_block(kb, unused):
            at = rows + kb * width
            allowed = (at >= first) & (at <= last)
            for h in range(UNITS):
                scores = over_rows(kv[kb, head_rows(h), :], q[j, head_rows(h), :])
                scores = jnp.where(allowed, scores, NEG)
                before = top[h : h + 1, :]
                peak = jnp.maximum(before, jnp.max(scores, axis=0, keepdims=True))
                expo = jnp.exp(scores - peak)
                shrink = jnp.exp(before - peak)
                top[h : h + 1, :] = peak
                total[h : h + 1, :] = total[h : h + 1, :] * shrink + jnp.sum(
                    expo, axis=0, keepdims=True
                )
                accum[head_rows(h), :] = accum[head_rows(h), :] * shrink + jnp.dot(
                    kv[kb, head_rows(h, R), :],
                    expo.astype(jnp.bfloat16),
                    preferred_element_type=jnp.float32,
                )
            return unused

        stop = jnp.minimum(own, (length + width - 1) // width)
        lax.fori_loop(info[j], stop, one_key_block, 0)
        for h in range(UNITS):
            result = accum[head_rows(h), :] / total[h : h + 1, :]
            out_wide[j, head_rows(h), :] = result
            out_low[j, head_rows(h), :] = result.astype(jnp.bfloat16)
            logs[j, h : h + 1, :] = top[h : h + 1, :] + jnp.log(total[h : h + 1, :])
        return unused

    lax.fori_loop(0, CHIPS, one_query_block, 0)


def attention_forward(info, q, kv, lo, halo):
    width = q.shape[2]
    return pl.pallas_call(
        functools.partial(forward_kernel, halo),
        name="attention_forward",
        out_shape=(
            jax.ShapeDtypeStruct((CHIPS, R, width), jnp.float32),
            jax.ShapeDtypeStruct((CHIPS, R, width), jnp.bfloat16),
            jax.ShapeDtypeStruct((CHIPS, 8, width), jnp.float32),
        ),
        in_specs=[SMEM, VMEM, VMEM, VMEM],
        out_specs=(VMEM, VMEM, VMEM),
        scratch_shapes=[
            pltpu.VMEM((8, width), jnp.float32),
            pltpu.VMEM((8, width), jnp.float32),
            pltpu.VMEM((R, width), jnp.float32),
        ],
        compiler_params=pltpu.CompilerParams(vmem_limit_bytes=48 << 20),
    )(info, q, kv, lo)


def backward_kernel(halo, info, q, kv, lo, grad, wide, logs, dq, dkv, query_acc, deltas):
    width = q.shape[2]
    core, length = info[CHIPS], info[CHIPS + 1]
    rows = lax.broadcasted_iota(jnp.int32, (width, width), 0)
    columns = lax.broadcasted_iota(jnp.int32, (1, width), 1)
    dkv[...] = jnp.zeros_like(dkv)

    def one_query_block(j, unused):
        own = halo + 2 * j + core
        position = own * width + columns
        first = lo[j, 0:1, :]
        last = jnp.minimum(position, length - 1)
        for h in range(UNITS):
            deltas[h : h + 1, :] = jnp.sum(
                grad[j, head_rows(h), :].astype(jnp.float32) * wide[j, head_rows(h), :],
                axis=0,
                keepdims=True,
            )
        query_acc[...] = jnp.zeros_like(query_acc)

        def block(kb, allowed):
            for h in range(UNITS):
                key, value = kv[kb, head_rows(h), :], kv[kb, head_rows(h, R), :]
                query, wanted = q[j, head_rows(h), :], grad[j, head_rows(h), :]
                scores = over_rows(key, query)
                probs = jnp.where(allowed, jnp.exp(scores - logs[j, h : h + 1, :]), 0.0)
                grad_probs = over_rows(value, wanted)
                grad_scores = (probs * (grad_probs - deltas[h : h + 1, :])).astype(jnp.bfloat16)
                dkv[kb, head_rows(h, R), :] += over_lanes(wanted, probs.astype(jnp.bfloat16))
                dkv[kb, head_rows(h), :] += over_lanes(query, grad_scores)
                query_acc[head_rows(h), :] += jnp.dot(
                    key, grad_scores, preferred_element_type=jnp.float32
                )

        diag = rows + own * width
        block(own, ((diag >= first) & (diag <= last)) | (diag == position))

        def one_key_block(kb, unused):
            at = rows + kb * width
            block(kb, (at >= first) & (at <= last))
            return unused

        stop = jnp.minimum(own, (length + width - 1) // width)
        lax.fori_loop(info[j], stop, one_key_block, 0)
        dq[j] = (query_acc[...] * HEAD ** (-0.5)).astype(jnp.bfloat16)
        return unused

    lax.fori_loop(0, CHIPS, one_query_block, 0)


def attention_backward(info, q, kv, lo, grad, wide, logs, halo):
    width = q.shape[2]
    return pl.pallas_call(
        functools.partial(backward_kernel, halo),
        name="attention_backward",
        out_shape=(
            jax.ShapeDtypeStruct((CHIPS, R, width), jnp.bfloat16),
            jax.ShapeDtypeStruct((halo + GROUP, 2 * R, width), jnp.float32),
        ),
        in_specs=[SMEM] + [VMEM] * 6,
        out_specs=(VMEM, VMEM),
        scratch_shapes=[
            pltpu.VMEM((R, width), jnp.float32),
            pltpu.VMEM((8, width), jnp.float32),
        ],
        compiler_params=pltpu.CompilerParams(vmem_limit_bytes=56 << 20),
    )(info, q, kv, lo, grad, wide, logs)


def as_terms(grad, chunks):
    return grad.astype(jnp.bfloat16).reshape(2, 2, chunks, -1, grad.shape[1])


def local(
    tokens,
    first_values,
    teacher,
    segment_ids,
    lengths,
    ln1_gain,
    ln1_bias,
    w_qkv,
    qv_bias,
    w_out,
    b_out,
    ln2_gain,
    ln2_bias,
    w_fc,
    b_fc,
    w_proj,
    b_proj,
):
    seq_count, width = tokens.shape[0], tokens.shape[1]
    row_count = seq_count * width
    ctx_size = lax.axis_size("ctx")
    ctx_index = lax.axis_index("ctx")
    groups = ctx_size // GROUP
    halo = pl.cdiv(DOC_MAX - 1, width) if groups > 1 else 0
    assert seq_count == SEQS and ctx_size % GROUP == 0 and halo <= GROUP
    chip, core = ctx_index % GROUP // 2, ctx_index % 2
    small_parts = (ln1_gain, ln1_bias, qv_bias, b_out, ln2_gain, ln2_bias, b_fc, b_proj)
    small_sizes = [part.shape[0] for part in small_parts]
    small_rows = pl.cdiv(sum(small_sizes), 2 * 16 * 128) * 16
    packed = jnp.concatenate(small_parts)
    packed = jnp.pad(packed, (0, 2 * small_rows * 128 - packed.shape[0]))
    qkv_full, small_full = gather_first(
        w_qkv.reshape(2, 4, w_qkv.shape[0] // 8, -1), packed.reshape(2, 1, small_rows, 128)
    )
    qkv_weight = qkv_full.reshape(D, -1)
    small_full = small_full.reshape(2, -1)
    vectors, at = [], 0
    for size in small_sizes:
        vectors.append(small_full[:, at : at + size].reshape(-1))
        at += size
    (
        norm1_gain,
        norm1_shift,
        qv_shift,
        out_shift,
        norm2_gain,
        norm2_shift,
        fc_shift,
        proj_shift,
    ) = vectors
    query_pos = ctx_index * width + jnp.arange(width, dtype=jnp.int32)

    window = (halo + GROUP) * width
    start = ctx_index // GROUP * GROUP * width - halo * width
    ids = lax.dynamic_index_in_dim(segment_ids, chip // PER_SEQ, 0, keepdims=False)
    if halo:
        ids = jnp.concatenate([jnp.full((halo * width,), -1, jnp.int32), ids])
    ids = lax.dynamic_slice_in_dim(ids, start + halo * width, window, 0)
    mine = lax.dynamic_index_in_dim(
        ids[halo * width :].reshape(CHIPS, 2, width), core, 1, keepdims=False
    )
    lo = jnp.sum((ids[None, None, :] < mine[:, :, None]).astype(jnp.int32), axis=-1)
    length = lax.dynamic_index_in_dim(lengths, chip // PER_SEQ, 0, keepdims=False) - start
    info = jnp.concatenate([lo[:, 0] // width, jnp.stack([core, length])]).astype(jnp.int32)
    lo = jnp.broadcast_to(lo[:, None, :], (CHIPS, 8, width))

    inputs = tokens.reshape(row_count, D).astype(jnp.float32)
    normed1, norm1_back = jax.vjp(
        norm_layer, inputs, norm1_gain.astype(jnp.float32), norm1_shift.astype(jnp.float32)
    )
    normed1_low = normed1.astype(jnp.bfloat16)
    projected = lax.dot_general(
        qkv_weight, normed1_low, (((0,), (1,)), ((), ())), preferred_element_type=jnp.float32
    )
    shift_wide = qv_shift.astype(jnp.float32)[:, None]
    sent = jnp.concatenate(
        [
            (projected[:D] + shift_wide[:D]).astype(jnp.bfloat16) * HEAD ** (-0.5),
            projected[D : 2 * D].astype(jnp.bfloat16),
            (projected[2 * D :] + shift_wide[D:]).astype(jnp.bfloat16),
            first_values.reshape(row_count, D - VW).T,
        ],
        axis=0,
    )
    q_all, kv_all, out_full, fc_full = scatter_heads(
        sent,
        w_out.reshape(2, 1, w_out.shape[0] // 2, -1),
        w_fc.reshape(2, 4, w_fc.shape[0] // 8, -1),
        width,
    )
    out_weight, fc_weight = out_full.reshape(D, D), fc_full.reshape(D, -1)
    if halo:
        ahead = [(i, i + GROUP) for i in range(ctx_size - GROUP)]
        kv_all = jnp.concatenate(
            [lax.ppermute(kv_all[GROUP - halo :], "ctx", ahead), kv_all], axis=0
        )
    out_wide, out_low, logs = attention_forward(info, q_all, kv_all, lo, halo)
    attended, proj_full = send_home(out_low, w_proj.reshape(2, 4, w_proj.shape[0] // 8, -1))
    proj_weight = proj_full.reshape(-1, D)
    resid = inputs + over_rows(attended, out_weight) + out_shift.astype(jnp.float32)
    normed2, norm2_back = jax.vjp(
        norm_layer, resid, norm2_gain.astype(jnp.float32), norm2_shift.astype(jnp.float32)
    )
    normed2_low = normed2.astype(jnp.bfloat16)
    pre_act = jnp.dot(normed2_low, fc_weight, preferred_element_type=jnp.float32) + fc_shift.astype(
        jnp.float32
    )
    activ, gelu_back = jax.vjp(smooth_gate, pre_act)
    activ_low = activ.astype(jnp.bfloat16)
    result = (
        resid
        + jnp.dot(activ_low, proj_weight, preferred_element_type=jnp.float32)
        + proj_shift.astype(jnp.float32)
    )
    valid_rows = (query_pos[None, :] < lengths[:, None]).astype(jnp.float32)
    deviation = (
        result.reshape(seq_count, width, D) - teacher.astype(jnp.float32)
    ) * valid_rows[:, :, None]
    grad_output = deviation.reshape(row_count, D)
    grad_mixed = grad_output.astype(jnp.bfloat16)
    grad_proj_w = over_rows(activ_low, grad_mixed)
    grad_proj_b = jnp.sum(grad_mixed.astype(jnp.float32), axis=0)
    grad_activ = over_lanes(grad_mixed, proj_weight)
    grad_pre = gelu_back(grad_activ)[0].astype(jnp.bfloat16)
    grad_fc_w = over_rows(normed2_low, grad_pre)
    grad_fc_b = jnp.sum(grad_pre.astype(jnp.float32), axis=0)
    grad_normed2 = over_lanes(grad_pre, fc_weight)
    grad_resid_norm, grad_g2, grad_b2 = norm2_back(grad_normed2)
    grad_resid = grad_output + grad_resid_norm
    grad_branch = grad_resid.astype(jnp.bfloat16)
    grad_out_w = jnp.dot(attended, grad_branch, preferred_element_type=jnp.float32)
    grad_out_b = jnp.sum(grad_branch.astype(jnp.float32), axis=0)
    grad_attended = over_lanes(out_weight, grad_branch).astype(jnp.bfloat16)
    grad_all, proj_sum = send_away(grad_attended, as_terms(grad_proj_w, 4), width)
    dq, dkv = attention_backward(info, q_all, kv_all, lo, grad_all, out_wide, logs, halo)
    if halo:
        behind = [(i + GROUP, i) for i in range(ctx_size - GROUP)]
        over = lax.ppermute(dkv[:halo].astype(jnp.bfloat16), "ctx", behind)
        dkv = dkv[halo:].at[GROUP - halo :].add(over.astype(jnp.float32))
    grads_t, fc_sum, out_sum = return_heads(
        dq, dkv, as_terms(grad_fc_w, 4), as_terms(grad_out_w, 1)
    )
    grad_projected = grads_t[: 2 * D + VW]
    grad_first = grads_t[2 * D + VW :].T.astype(jnp.float32)
    grad_qkv_w = lax.dot_general(
        normed1_low, grad_projected, (((0,), (1,)), ((), ())), preferred_element_type=jnp.float32
    )
    grad_sums = jnp.sum(grad_projected.astype(jnp.float32), axis=1)
    grad_qv_b = jnp.concatenate([grad_sums[:D], grad_sums[2 * D :]])
    grad_normed1 = lax.dot_general(
        grad_projected, qkv_weight, (((0,), (1,)), ((), ())), preferred_element_type=jnp.float32
    )
    grad_input_norm, grad_g1, grad_b1 = norm1_back(grad_normed1)
    grad_inputs = grad_resid + grad_input_norm
    small_grads = (grad_g1, grad_b1, grad_qv_b, grad_out_b, grad_g2, grad_b2, grad_fc_b, grad_proj_b)
    small_grads = jnp.concatenate(
        [part.reshape(2, -1) for part in small_grads], axis=1
    ).reshape(-1)
    scalars = jnp.stack([jnp.sum(deviation * deviation), jnp.sum(valid_rows)])
    small_grads = jnp.concatenate([small_grads, scalars])
    total_rows = pl.cdiv(small_grads.shape[0], 8 * 128) * 8
    small_grads = jnp.pad(small_grads, (0, total_rows * 128 - small_grads.shape[0]))
    small_all, proj_all, fc_all, out_all, qkv_all = finish_sums(
        small_grads.reshape(total_rows, 128),
        [part.reshape(CHIPS, -1, part.shape[-1]) for part in (proj_sum, fc_sum, out_sum)],
        as_terms(grad_qkv_w, CHIPS),
    )
    small_all = small_all.reshape(-1)
    large = [part.reshape(-1, part.shape[-1]) for part in (qkv_all, out_all, fc_all, proj_all)]
    if groups > 1:
        sets = [[first + GROUP * g for g in range(groups)] for first in range(GROUP)]
        small_all = lax.psum(small_all, "ctx", axis_index_groups=sets)
        large = [
            lax.psum(part.astype(jnp.float32), "ctx", axis_index_groups=sets) for part in large
        ]
    large = [part.astype(jnp.float32) for part in large]
    length_all = sum(small_sizes)
    loss = small_all[2 * length_all] / (small_all[2 * length_all + 1] * D)
    my_small = lax.dynamic_slice_in_dim(
        small_all, lax.axis_index("wsh") * length_all, length_all
    )
    shares, at = [], 0
    for size in small_sizes:
        shares.append(my_small[at : at + size])
        at += size
    return (
        loss,
        result.reshape(seq_count, width, D).astype(jnp.bfloat16),
        grad_inputs.reshape(seq_count, width, D),
        grad_first.reshape(seq_count, width, D - VW),
        shares[0],
        shares[1],
        large[0],
        shares[2],
        large[1],
        shares[3],
        shares[4],
        shares[5],
        large[2],
        shares[6],
        large[3],
        shares[7],
    )


def solution(mesh):
    whole, rows, vector = P("wsh", "ctx", None), P("wsh", None), P("wsh")
    in_specs = (whole, whole, whole, rows, vector) + (
        vector,
        vector,
        rows,
        vector,
        rows,
        vector,
        vector,
        vector,
        rows,
        vector,
        rows,
        vector,
    )
    out_specs = (P(), whole, whole, whole) + in_specs[5:]
    return jax.shard_map(local, mesh=mesh, in_specs=in_specs, out_specs=out_specs, check_vma=False)
```

```python
import functools

import jax
import jax.numpy as jnp
from jax import lax
from jax.experimental import pallas as pl
from jax.experimental.pallas import tpu as pltpu
from jax.sharding import PartitionSpec as P

D = 768
HEADS = 12
HEAD = 64
DOC_MAX = 2048
VW = 384

EPS = 1e-05
NEG = -1e30

CHIPS = 8
GROUP = 2 * CHIPS
SEQS = 2
PER_SEQ = CHIPS // SEQS
UNITS = SEQS * HEADS // CHIPS
R = UNITS * HEAD
MESH = pl.DeviceIdType.MESH
DMA = pltpu.SemaphoreType.DMA


def norm_layer(values, gain_vec, offset):
    average = jnp.mean(values, axis=-1, keepdims=True)
    centred = values - average
    variance = jnp.mean(centred * centred, axis=-1, keepdims=True)
    return centred * lax.rsqrt(variance + EPS) * gain_vec + offset


def smooth_gate(values):
    return jax.nn.gelu(values, approximate=True)


def where_am_i():
    index, wsh = lax.axis_index("ctx"), lax.axis_index("wsh")
    base = index // GROUP * GROUP
    chip, core = index % GROUP // 2, index % 2

    def same_core(other):
        return (base + 2 * other + core, wsh)

    sibling, partner = (base + 2 * chip + 1 - core, wsh), (index, 1 - wsh)
    return chip, core, same_core, sibling, partner, wsh


def greet(peers):
    barrier = pltpu.get_barrier_semaphore()
    for peer in peers:
        pl.semaphore_signal(barrier, inc=1, device_id=peer, device_id_type=MESH)
    pl.semaphore_wait(barrier, len(peers))


def remote(src, dst, send, recv, peer):
    return pltpu.make_async_remote_copy(
        src_ref=src, dst_ref=dst, send_sem=send, recv_sem=recv, device_id=peer, device_id_type=MESH
    )


def lanes_of(chip, width):
    return pl.ds(pl.multiple_of(chip // PER_SEQ * width, width), width)


def rows_of(chip, first):
    return pl.ds(pl.multiple_of(first + chip % PER_SEQ * R, R), R)


def share_start(shard, full, sems, sibling, partner, core, wsh):
    xs, xr, fs, fr, own_send, own_recv = sems
    sends = []
    for k in range(shard.shape[1]):
        sends.append(remote(shard.at[core, k], full.at[wsh, core, k], xs.at[k], xr.at[k], partner))
        sends[-1].start()
    same = remote(shard, full.at[wsh], own_send, own_recv, sibling)
    same.start()
    return sends, same


def share_pass(state, k, full, sems, sibling, core, wsh):
    xs, xr, fs, fr, own_send, own_recv = sems
    state[0][k].wait_recv()
    piece = full.at[1 - wsh, core, k]
    forward = remote(piece, piece, fs.at[k], fr.at[k], sibling)
    forward.start()
    return forward


def share_end(state, forwards):
    state[1].wait()
    for copy in state[0]:
        copy.wait_send()
    for copy in forwards:
        copy.wait()


def share_scratch(shard):
    chunks = shard.shape[1]
    return [DMA((chunks,)), DMA((chunks,)), DMA((chunks,)), DMA((chunks,)), DMA, DMA]


def full_of(shard):
    return jax.ShapeDtypeStruct((2,) + shard.shape, shard.dtype)


def first_kernel(weight, small, full, all_small, *sems):
    chip, core, same_core, sibling, partner, wsh = where_am_i()
    greet([sibling, partner])
    pack = share_start(small, all_small, sems[6:], sibling, partner, core, wsh)
    state = share_start(weight, full, sems[:6], sibling, partner, core, wsh)
    passed = [share_pass(pack, 0, all_small, sems[6:], sibling, core, wsh)]
    forwards = [
        share_pass(state, k, full, sems[:6], sibling, core, wsh) for k in range(weight.shape[1])
    ]
    share_end(pack, passed)
    share_end(state, forwards)


def scatter_kernel(src, *refs):
    chip, core, same_core, sibling, partner, wsh = where_am_i()
    weights, (q_all, kv_all), fulls, refs = refs[:3], refs[3:5], refs[5:8], refs[8:]
    send, recv, fsend, frecv, own = refs[:5]
    sems = [refs[5 + 6 * n : 11 + 6 * n] for n in range(3)]
    width = q_all.shape[2]
    greet([same_core((chip + i) % CHIPS) for i in range(1, CHIPS)] + [sibling, partner])
    block = 2 * chip + core

    def pieces(target):
        lanes = lanes_of(target, width)
        return (
            (src.at[rows_of(target, D), lanes], kv_all.at[block, pl.ds(0, R)]),
            (src.at[rows_of(target, 2 * D), lanes], kv_all.at[block, pl.ds(R, R)]),
            (src.at[rows_of(target, 0), lanes], q_all.at[chip]),
        )

    copies = []
    for i in range(1, CHIPS):
        target = (chip + i) % CHIPS
        copies.append(
            [
                remote(a, b, send.at[n, i], recv.at[n, i], same_core(target))
                for n, (a, b) in enumerate(pieces(target))
            ]
        )
        for copy in copies[-1]:
            copy.start()
    local = [pltpu.make_async_copy(a, b, own.at[n]) for n, (a, b) in enumerate(pieces(chip))]
    for copy in local:
        copy.start()
    states = [
        share_start(weights[n], fulls[n], sems[n], sibling, partner, core, wsh) for n in range(3)
    ]
    for copy in local:
        copy.wait()
    forwards = []
    for i in range(CHIPS):
        if i:
            copies[i - 1][0].wait_recv()
            copies[i - 1][1].wait_recv()
        came = 2 * ((chip + CHIPS - i) % CHIPS) + core
        forwards.append(remote(kv_all.at[came], kv_all.at[came], fsend.at[i], frecv.at[i], sibling))
        forwards[-1].start()
    passed = [
        [
            share_pass(states[n], k, fulls[n], sems[n], sibling, core, wsh)
            for k in range(weights[n].shape[1])
        ]
        for n in range(3)
    ]
    for i in range(1, CHIPS):
        copies[i - 1][2].wait_recv()
    for batch in copies:
        for copy in batch:
            copy.wait_send()
    for copy in forwards:
        copy.wait()
    for n in range(3):
        share_end(states[n], passed[n])


def home_kernel(src, dst, send, recv, own):
    chip, core, same_core, sibling, partner, wsh = where_am_i()
    width = src.shape[2]
    greet([same_core((chip + i) % CHIPS) for i in range(1, CHIPS)])
    place = dst.at[rows_of(chip, 0), lanes_of(chip, width)]
    copies = []
    for i in range(1, CHIPS):
        target = (chip + i) % CHIPS
        copies.append(remote(src.at[target], place, send.at[i], recv.at[i], same_core(target)))
        copies[-1].start()
    local = pltpu.make_async_copy(src.at[chip], place, own)
    local.start()
    local.wait()
    for copy in copies:
        copy.wait()


def add_into(dst, parts):
    rows = dst.shape[0]
    step = 16 if rows % 16 == 0 else 8

    def one(i, unused):
        at = pl.ds(pl.multiple_of(i * step, step), step)
        total = parts[0][at, :].astype(jnp.float32)
        for part in parts[1:]:
            total = total + part[at, :].astype(jnp.float32)
        dst[at, :] = total.astype(dst.dtype)
        return unused

    lax.fori_loop(0, rows // step, one, 0)


def pair_start(terms, buffers, sems, sibling, core, wsh):
    from_sibling, for_partner, from_partner = buffers
    ss, sr, xs, xr = sems
    gives = []
    for half in range(2):
        which = 1 - wsh if half == 0 else wsh
        for k in range(terms.shape[2]):
            gives.append(
                remote(
                    terms.at[which, 1 - core, k],
                    from_sibling.at[half, k],
                    ss.at[half, k],
                    sr.at[half, k],
                    sibling,
                )
            )
            gives[-1].start()
    return gives


def pair_cross(terms, buffers, sems, gives, partner, core, wsh):
    from_sibling, for_partner, from_partner = buffers
    ss, sr, xs, xr = sems
    sends = []
    for k in range(terms.shape[2]):
        gives[k].wait_recv()
        add_into(for_partner.at[k], [terms.at[1 - wsh, core, k], from_sibling.at[0, k]])
        sends.append(remote(for_partner.at[k], from_partner.at[k], xs.at[k], xr.at[k], partner))
        sends[-1].start()
    return sends


def pair_end(terms, buffers, gives, sends, result, core, wsh):
    from_sibling, for_partner, from_partner = buffers
    chunks = terms.shape[2]
    for k in range(chunks):
        gives[chunks + k].wait_recv()
        sends[k].wait_recv()
        add_into(
            result.at[k], [terms.at[wsh, core, k], from_sibling.at[1, k], from_partner.at[k]]
        )
    for copy in gives + sends:
        copy.wait_send()


def pair_scratch(terms):
    chunks, rows, columns = terms.shape[2:]
    return [
        pltpu.VMEM((2, chunks, rows, columns), jnp.bfloat16),
        pltpu.VMEM((chunks, rows, columns), jnp.bfloat16),
        pltpu.VMEM((chunks, rows, columns), jnp.bfloat16),
        DMA((2, chunks)),
        DMA((2, chunks)),
        DMA((chunks,)),
        DMA((chunks,)),
    ]


def away_kernel(src, dst, send, recv, own):
    chip, core, same_core, sibling, partner, wsh = where_am_i()
    width = dst.shape[2]
    greet([same_core((chip + i) % CHIPS) for i in range(1, CHIPS)])
    copies = []
    for i in range(1, CHIPS):
        target = (chip + i) % CHIPS
        piece = src.at[rows_of(target, 0), lanes_of(target, width)]
        copies.append(remote(piece, dst.at[chip], send.at[i], recv.at[i], same_core(target)))
        copies[-1].start()
    local = pltpu.make_async_copy(
        src.at[rows_of(chip, 0), lanes_of(chip, width)], dst.at[chip], own
    )
    local.start()
    local.wait()
    for copy in copies:
        copy.wait()


def return_kernel(dq, dkv, *refs):
    chip, core, same_core, sibling, partner, wsh = where_am_i()
    terms, dst, results, refs = refs[:3], refs[3], refs[4:7], refs[7:]
    give, take, final, send, recv, fsend, frecv, own = refs[:8]
    pairs = [refs[8 + 7 * n : 15 + 7 * n] for n in range(3)]
    width = dq.shape[2]
    greet([same_core((chip + i) % CHIPS) for i in range(1, CHIPS)] + [sibling, partner])
    lanes = lanes_of(chip, width)
    halves = []
    for i in range(CHIPS):
        target = (chip + i) % CHIPS
        give[target] = dkv[2 * target + 1 - core].astype(jnp.bfloat16)
        halves.append(
            remote(give.at[target], take.at[target], fsend.at[i], frecv.at[i], sibling)
        )
        halves[-1].start()
    copies = []
    for i in range(1, CHIPS):
        target = (chip + i) % CHIPS
        copies.append(
            remote(
                dq.at[target],
                dst.at[rows_of(chip, 0), lanes],
                send.at[0, i],
                recv.at[0, i],
                same_core(target),
            )
        )
        copies[-1].start()
    local = [pltpu.make_async_copy(dq.at[chip], dst.at[rows_of(chip, 0), lanes], own.at[0])]
    local[0].start()
    gives = [pair_start(terms[n], pairs[n][:3], pairs[n][3:], sibling, core, wsh) for n in range(3)]
    for i in list(range(1, CHIPS)) + [0]:
        target = (chip + i) % CHIPS
        halves[i].wait_recv()
        final[target] = (dkv[2 * target + core] + take[target].astype(jnp.float32)).astype(
            jnp.bfloat16
        )
        for n in (1, 2):
            piece = final.at[target, pl.ds((n - 1) * R, R)]
            place = dst.at[rows_of(chip, n * D), lanes]
            if i:
                copies.append(
                    remote(piece, place, send.at[n, i], recv.at[n, i], same_core(target))
                )
                copies[-1].start()
            else:
                local.append(pltpu.make_async_copy(piece, place, own.at[n]))
                local[-1].start()
    sends = [
        pair_cross(terms[n], pairs[n][:3], pairs[n][3:], gives[n], partner, core, wsh)
        for n in range(3)
    ]
    for n in range(3):
        pair_end(terms[n], pairs[n][:3], gives[n], sends[n], results[n], core, wsh)
    for copy in local:
        copy.wait()
    for copy in halves:
        copy.wait_send()
    for copy in copies:
        copy.wait()


CUT = 24


def cuts_of(shapes):
    cuts = []
    for n, (pieces, rows, columns) in enumerate(shapes):
        width = next(w for w in (768, 640, columns) if columns % w == 0)
        cuts += [
            (n, row, column, width)
            for row in range(0, rows, CUT)
            for column in range(0, columns, width)
        ]
    return cuts


def finish_kernel(cuts, small, *refs):
    chip, core, same_core, sibling, partner, wsh = where_am_i()
    sums, terms = refs[:3], refs[3]
    all_small, outs = refs[4], refs[5:9]
    kept, pair, refs = refs[9], refs[10:17], refs[17:]
    small_take, small_send, small_recv, refs = refs[0], refs[1], refs[2], refs[3:]
    took_b, added, took_a = refs[: len(cuts)], refs[len(cuts) : 2 * len(cuts)], refs[2 * len(cuts) :]
    took_a, (bs, br, zs, zr, gs, gr, hs, hr, ks, kr) = took_a[: len(cuts)], took_a[len(cuts) :]
    a, b = chip // 2, chip % 2
    along_a = [(a + i) % 4 for i in range(4)]
    other_b = same_core(2 * a + 1 - b)
    peers_a = [same_core(2 * other + b) for other in along_a]
    greet([sibling, partner, other_b] + peers_a[1:])
    mine = list(sums) + [kept]
    here, there = pl.multiple_of(4 * b, 4), pl.multiple_of(4 - 4 * b, 4)
    flying = []

    def go(*args):
        copy = remote(*args)
        copy.start()
        flying.append(copy)
        return copy

    def whole(n, *where):
        ref, row, column, width = (outs, mine)[len(where) == 1][cuts[n][0]], *cuts[n][1:]
        return ref.at[(*where, pl.ds(row, CUT), pl.ds(column, width))]

    def swap(n):
        return go(whole(n, pl.ds(there, 4)), took_b[n], bs.at[n], br.at[n], other_b)

    def spread(n, copy):
        copy.wait_recv()
        copies = []
        for i in (2, 1, 3, 0):
            other = along_a[i]
            add_into(added[n].at[other], [whole(n, here + other), took_b[n].at[other]])
            if i:
                copies.append(
                    go(
                        added[n].at[other],
                        took_a[n].at[i - 1],
                        zs.at[n, i - 1],
                        zr.at[n, i - 1],
                        peers_a[i],
                    )
                )
        return copies

    def give(n, copies):
        for copy in copies:
            copy.wait_recv()
        piece = whole(n, core, here + a)
        add_into(piece, [added[n].at[a]] + [took_a[n].at[i] for i in range(3)])
        return [
            go(piece, piece, gs.at[n, i - 1], gr.at[n, i - 1], peers_a[i]) for i in (2, 1, 3)
        ]

    def cross(n, copies):
        for copy in copies:
            copy.wait_recv()
        half = whole(n, core, pl.ds(here, 4))
        copies = [go(half, half, hs.at[n], hr.at[n], other_b)]
        return copies + [go(half, half, ks.at[n, 0], kr.at[n, 0], sibling)]

    def close(n, copies):
        copies[0].wait_recv()
        half = whole(n, core, pl.ds(there, 4))
        return [copies[1], go(half, half, ks.at[n, 1], kr.at[n, 1], sibling)]

    def small_start(n):
        if n < 3:
            small_take[3 + n] = all_small[...]
            peer = (sibling, partner, other_b)[n]
            place = small_take.at[3 + n], small_take.at[n], small_send.at[n], small_recv.at[n]
            return [go(*place, peer)]
        place = small_take.at[6 + a]
        place[...] = all_small[...]
        return [
            go(place, place, small_send.at[2 + i], small_recv.at[2 + i], peers_a[i])
            for i in (1, 2, 3)
        ]

    def small_end(n, copies):
        for copy in copies:
            copy.wait_recv()
        if n < 3:
            all_small[...] = all_small[...] + small_take[n]
        else:
            all_small[...] = (small_take[6] + small_take[7]) + (small_take[8] + small_take[9])

    gives = pair_start(terms, pair[:3], pair[3:], sibling, core, wsh)
    state = {0: swap(0), 1: swap(1)}
    all_small[...] = small[...]
    small_copies = small_start(0)
    sends = pair_cross(terms, pair[:3], pair[3:], gives, partner, core, wsh)
    late = next(n for n, cut in enumerate(cuts) if cut[0] == 3)
    for tick in range(len(cuts) + 4):
        if tick == late - 2:
            pair_end(terms, pair[:3], gives, sends, kept, core, wsh)
        if 2 <= tick + 2 < len(cuts):
            state[tick + 2] = swap(tick + 2)
        for lag, stage in enumerate((spread, give, cross, close)):
            if 0 <= tick - lag < len(cuts):
                state[tick - lag] = stage(tick - lag, state[tick - lag])
        if tick < 4:
            small_end(tick, small_copies)
            if tick < 3:
                small_copies = small_start(tick + 1)
    for n in range(len(cuts)):
        for copy in state[n]:
            copy.wait_recv()
    for copy in flying:
        copy.wait_send()


ANY = pl.BlockSpec(memory_space=pl.ANY)
VMEM = pl.BlockSpec(memory_space=pltpu.VMEM)
SMEM = pl.BlockSpec(memory_space=pltpu.SMEM)


def comm_params(number, mib=48):
    return pltpu.CompilerParams(
        collective_id=number, has_side_effects=True, vmem_limit_bytes=mib << 20
    )


def gather_first(weight, small):
    return pl.pallas_call(
        first_kernel,
        name="gather_first",
        out_shape=(full_of(weight), full_of(small)),
        in_specs=[ANY, ANY],
        out_specs=(ANY, ANY),
        scratch_shapes=share_scratch(weight) + share_scratch(small),
        compiler_params=comm_params(4),
    )(weight, small)


def scatter_heads(src, weights, width):
    return pl.pallas_call(
        scatter_kernel,
        name="scatter_heads",
        out_shape=[
            jax.ShapeDtypeStruct((CHIPS, R, width), jnp.bfloat16),
            jax.ShapeDtypeStruct((GROUP, 2 * R, width), jnp.bfloat16),
        ]
        + [full_of(weight) for weight in weights],
        in_specs=[ANY] * 4,
        out_specs=[ANY] * 5,
        scratch_shapes=[
            DMA((3, CHIPS)),
            DMA((3, CHIPS)),
            DMA((CHIPS,)),
            DMA((CHIPS,)),
            DMA((3,)),
        ]
        + [item for weight in weights for item in share_scratch(weight)],
        compiler_params=comm_params(0),
    )(src, *weights)


def send_home(src):
    width = src.shape[2]
    return pl.pallas_call(
        home_kernel,
        name="send_home",
        out_shape=jax.ShapeDtypeStruct((D, SEQS * width), jnp.bfloat16),
        in_specs=[ANY],
        out_specs=ANY,
        scratch_shapes=[DMA((CHIPS,)), DMA((CHIPS,)), DMA],
        compiler_params=comm_params(1),
    )(src)


def sum_of(terms):
    return jax.ShapeDtypeStruct(terms.shape[2:], jnp.bfloat16)


def send_away(src, width):
    return pl.pallas_call(
        away_kernel,
        name="send_away",
        out_shape=jax.ShapeDtypeStruct((CHIPS, R, width), jnp.bfloat16),
        in_specs=[ANY],
        out_specs=ANY,
        scratch_shapes=[DMA((CHIPS,)), DMA((CHIPS,)), DMA],
        compiler_params=comm_params(2),
    )(src)


def return_heads(dq, dkv, terms):
    width = dq.shape[2]
    pair = pltpu.VMEM((CHIPS, 2 * R, width), jnp.bfloat16)
    return pl.pallas_call(
        return_kernel,
        name="return_heads",
        out_shape=[jax.ShapeDtypeStruct((3 * D, SEQS * width), jnp.bfloat16)]
        + [sum_of(part) for part in terms],
        in_specs=[ANY] + [VMEM] * 4,
        out_specs=[ANY] + [VMEM] * 3,
        scratch_shapes=[
            pair,
            pair,
            pair,
            DMA((3, CHIPS)),
            DMA((3, CHIPS)),
            DMA((CHIPS,)),
            DMA((CHIPS,)),
            DMA((3,)),
        ]
        + [item for part in terms for item in pair_scratch(part)],
        compiler_params=comm_params(3, 56),
    )(dq, dkv, *terms)


def finish_sums(small, sums, terms):
    kept = sum_of(terms)
    whole = [*sums, kept]
    cuts = cuts_of([total.shape for total in whole])
    count = len(cuts)
    return pl.pallas_call(
        functools.partial(finish_kernel, cuts),
        name="finish_sums",
        out_shape=[jax.ShapeDtypeStruct(small.shape, small.dtype)]
        + [jax.ShapeDtypeStruct((2,) + total.shape, total.dtype) for total in whole],
        in_specs=[VMEM] * 5,
        out_specs=[VMEM] * 5,
        scratch_shapes=[pltpu.VMEM(kept.shape, kept.dtype)]
        + pair_scratch(terms)
        + [pltpu.VMEM((10,) + small.shape, small.dtype), DMA((6,)), DMA((6,))]
        + [pltpu.VMEM((4, CUT, cut[3]), jnp.bfloat16) for cut in cuts] * 2
        + [pltpu.VMEM((3, CUT, cut[3]), jnp.bfloat16) for cut in cuts]
        + [DMA((count,)), DMA((count,))]
        + [DMA((count, 3)) for _ in range(4)]
        + [DMA((count,)), DMA((count,))]
        + [DMA((count, 2)), DMA((count, 2))],
        compiler_params=comm_params(5, 56),
    )(small, *sums, terms)


def over_rows(left, right):
    return lax.dot_general(
        left, right, (((0,), (0,)), ((), ())), preferred_element_type=jnp.float32
    )


def over_lanes(left, right):
    return lax.dot_general(
        left, right, (((1,), (1,)), ((), ())), preferred_element_type=jnp.float32
    )


def head_rows(h, first=0):
    return slice(first + h * HEAD, first + (h + 1) * HEAD)


def forward_kernel(halo, info, q, kv, lo, out_wide, out_low, logs, top, total, accum):
    width = q.shape[2]
    core, length = info[CHIPS], info[CHIPS + 1]
    rows = lax.broadcasted_iota(jnp.int32, (width, width), 0)
    columns = lax.broadcasted_iota(jnp.int32, (1, width), 1)

    def one_query_block(j, unused):
        own = halo + 2 * j + core
        position = own * width + columns
        first = lo[j, 0:1, :]
        last = jnp.minimum(position, length - 1)

        diag = rows + own * width
        allowed = ((diag >= first) & (diag <= last)) | (diag == position)
        for h in range(UNITS):
            scores = over_rows(kv[own, head_rows(h), :], q[j, head_rows(h), :])
            scores = jnp.where(allowed, scores, NEG)
            peak = jnp.max(scores, axis=0, keepdims=True)
            expo = jnp.exp(scores - peak)
            top[h : h + 1, :] = peak
            total[h : h + 1, :] = jnp.sum(expo, axis=0, keepdims=True)
            accum[head_rows(h), :] = jnp.dot(
                kv[own, head_rows(h, R), :],
                expo.astype(jnp.bfloat16),
                preferred_element_type=jnp.float32,
            )

        def one_key_block(kb, unused):
            at = rows + kb * width
            allowed = (at >= first) & (at <= last)
            for h in range(UNITS):
                scores = over_rows(kv[kb, head_rows(h), :], q[j, head_rows(h), :])
                scores = jnp.where(allowed, scores, NEG)
                before = top[h : h + 1, :]
                peak = jnp.maximum(before, jnp.max(scores, axis=0, keepdims=True))
                expo = jnp.exp(scores - peak)
                shrink = jnp.exp(before - peak)
                top[h : h + 1, :] = peak
                total[h : h + 1, :] = total[h : h + 1, :] * shrink + jnp.sum(
                    expo, axis=0, keepdims=True
                )
                accum[head_rows(h), :] = accum[head_rows(h), :] * shrink + jnp.dot(
                    kv[kb, head_rows(h, R), :],
                    expo.astype(jnp.bfloat16),
                    preferred_element_type=jnp.float32,
                )
            return unused

        stop = jnp.minimum(own, (length + width - 1) // width)
        lax.fori_loop(info[j], stop, one_key_block, 0)
        for h in range(UNITS):
            result = accum[head_rows(h), :] / total[h : h + 1, :]
            out_wide[j, head_rows(h), :] = result
            out_low[j, head_rows(h), :] = result.astype(jnp.bfloat16)
            logs[j, h : h + 1, :] = top[h : h + 1, :] + jnp.log(total[h : h + 1, :])
        return unused

    lax.fori_loop(0, CHIPS, one_query_block, 0)


def attention_forward(info, q, kv, lo, halo):
    width = q.shape[2]
    return pl.pallas_call(
        functools.partial(forward_kernel, halo),
        name="attention_forward",
        out_shape=(
            jax.ShapeDtypeStruct((CHIPS, R, width), jnp.float32),
            jax.ShapeDtypeStruct((CHIPS, R, width), jnp.bfloat16),
            jax.ShapeDtypeStruct((CHIPS, 8, width), jnp.float32),
        ),
        in_specs=[SMEM, VMEM, VMEM, VMEM],
        out_specs=(VMEM, VMEM, VMEM),
        scratch_shapes=[
            pltpu.VMEM((8, width), jnp.float32),
            pltpu.VMEM((8, width), jnp.float32),
            pltpu.VMEM((R, width), jnp.float32),
        ],
        compiler_params=pltpu.CompilerParams(vmem_limit_bytes=48 << 20),
    )(info, q, kv, lo)


def backward_kernel(halo, info, q, kv, lo, grad, wide, logs, dq, dkv, query_acc, deltas):
    width = q.shape[2]
    core, length = info[CHIPS], info[CHIPS + 1]
    rows = lax.broadcasted_iota(jnp.int32, (width, width), 0)
    columns = lax.broadcasted_iota(jnp.int32, (1, width), 1)
    dkv[...] = jnp.zeros_like(dkv)

    def one_query_block(j, unused):
        own = halo + 2 * j + core
        position = own * width + columns
        first = lo[j, 0:1, :]
        last = jnp.minimum(position, length - 1)
        for h in range(UNITS):
            deltas[h : h + 1, :] = jnp.sum(
                grad[j, head_rows(h), :].astype(jnp.float32) * wide[j, head_rows(h), :],
                axis=0,
                keepdims=True,
            )
        query_acc[...] = jnp.zeros_like(query_acc)

        def block(kb, allowed):
            for h in range(UNITS):
                key, value = kv[kb, head_rows(h), :], kv[kb, head_rows(h, R), :]
                query, wanted = q[j, head_rows(h), :], grad[j, head_rows(h), :]
                scores = over_rows(key, query)
                probs = jnp.where(allowed, jnp.exp(scores - logs[j, h : h + 1, :]), 0.0)
                grad_probs = over_rows(value, wanted)
                grad_scores = (probs * (grad_probs - deltas[h : h + 1, :])).astype(jnp.bfloat16)
                dkv[kb, head_rows(h, R), :] += over_lanes(wanted, probs.astype(jnp.bfloat16))
                dkv[kb, head_rows(h), :] += over_lanes(query, grad_scores)
                query_acc[head_rows(h), :] += jnp.dot(
                    key, grad_scores, preferred_element_type=jnp.float32
                )

        diag = rows + own * width
        block(own, ((diag >= first) & (diag <= last)) | (diag == position))

        def one_key_block(kb, unused):
            at = rows + kb * width
            block(kb, (at >= first) & (at <= last))
            return unused

        stop = jnp.minimum(own, (length + width - 1) // width)
        lax.fori_loop(info[j], stop, one_key_block, 0)
        dq[j] = (query_acc[...] * HEAD ** (-0.5)).astype(jnp.bfloat16)
        return unused

    lax.fori_loop(0, CHIPS, one_query_block, 0)


def attention_backward(info, q, kv, lo, grad, wide, logs, halo):
    width = q.shape[2]
    return pl.pallas_call(
        functools.partial(backward_kernel, halo),
        name="attention_backward",
        out_shape=(
            jax.ShapeDtypeStruct((CHIPS, R, width), jnp.bfloat16),
            jax.ShapeDtypeStruct((halo + GROUP, 2 * R, width), jnp.float32),
        ),
        in_specs=[SMEM] + [VMEM] * 6,
        out_specs=(VMEM, VMEM),
        scratch_shapes=[
            pltpu.VMEM((R, width), jnp.float32),
            pltpu.VMEM((8, width), jnp.float32),
        ],
        compiler_params=pltpu.CompilerParams(vmem_limit_bytes=56 << 20),
    )(info, q, kv, lo, grad, wide, logs)


def as_terms(grad, chunks):
    return grad.astype(jnp.bfloat16).reshape(2, 2, chunks, -1, grad.shape[1])


def local(
    tokens,
    first_values,
    teacher,
    segment_ids,
    lengths,
    ln1_gain,
    ln1_bias,
    w_qkv,
    qv_bias,
    w_out,
    b_out,
    ln2_gain,
    ln2_bias,
    w_fc,
    b_fc,
    w_proj,
    b_proj,
):
    seq_count, width = tokens.shape[0], tokens.shape[1]
    row_count = seq_count * width
    ctx_size = lax.axis_size("ctx")
    ctx_index = lax.axis_index("ctx")
    groups = ctx_size // GROUP
    halo = pl.cdiv(DOC_MAX - 1, width) if groups > 1 else 0
    assert seq_count == SEQS and ctx_size % GROUP == 0 and halo <= GROUP
    chip, core = ctx_index % GROUP // 2, ctx_index % 2
    small_parts = (ln1_gain, ln1_bias, qv_bias, b_out, ln2_gain, ln2_bias, b_fc, b_proj)
    small_sizes = [part.shape[0] for part in small_parts]
    small_rows = pl.cdiv(sum(small_sizes), 2 * 16 * 128) * 16
    packed = jnp.concatenate(small_parts)
    packed = jnp.pad(packed, (0, 2 * small_rows * 128 - packed.shape[0]))
    qkv_full, small_full = gather_first(
        w_qkv.reshape(2, 4, w_qkv.shape[0] // 8, -1), packed.reshape(2, 1, small_rows, 128)
    )
    qkv_weight = qkv_full.reshape(D, -1)
    small_full = small_full.reshape(2, -1)
    vectors, at = [], 0
    for size in small_sizes:
        vectors.append(small_full[:, at : at + size].reshape(-1))
        at += size
    (
        norm1_gain,
        norm1_shift,
        qv_shift,
        out_shift,
        norm2_gain,
        norm2_shift,
        fc_shift,
        proj_shift,
    ) = vectors
    query_pos = ctx_index * width + jnp.arange(width, dtype=jnp.int32)

    window = (halo + GROUP) * width
    start = ctx_index // GROUP * GROUP * width - halo * width
    ids = lax.dynamic_index_in_dim(segment_ids, chip // PER_SEQ, 0, keepdims=False)
    if halo:
        ids = jnp.concatenate([jnp.full((halo * width,), -1, jnp.int32), ids])
    ids = lax.dynamic_slice_in_dim(ids, start + halo * width, window, 0)
    mine = lax.dynamic_index_in_dim(
        ids[halo * width :].reshape(CHIPS, 2, width), core, 1, keepdims=False
    )
    lo = jnp.sum((ids[None, None, :] < mine[:, :, None]).astype(jnp.int32), axis=-1)
    length = lax.dynamic_index_in_dim(lengths, chip // PER_SEQ, 0, keepdims=False) - start
    info = jnp.concatenate([lo[:, 0] // width, jnp.stack([core, length])]).astype(jnp.int32)
    lo = jnp.broadcast_to(lo[:, None, :], (CHIPS, 8, width))

    inputs = tokens.reshape(row_count, D).astype(jnp.float32)
    normed1, norm1_back = jax.vjp(
        norm_layer, inputs, norm1_gain.astype(jnp.float32), norm1_shift.astype(jnp.float32)
    )
    normed1_low = normed1.astype(jnp.bfloat16)
    projected = lax.dot_general(
        qkv_weight, normed1_low, (((0,), (1,)), ((), ())), preferred_element_type=jnp.float32
    )
    shift_wide = qv_shift.astype(jnp.float32)[:, None]
    sent = jnp.concatenate(
        [
            (projected[:D] + shift_wide[:D]).astype(jnp.bfloat16) * HEAD ** (-0.5),
            projected[D : 2 * D].astype(jnp.bfloat16),
            (projected[2 * D :] + shift_wide[D:]).astype(jnp.bfloat16),
            first_values.reshape(row_count, D - VW).T,
        ],
        axis=0,
    )
    q_all, kv_all, out_full, fc_full, proj_full = scatter_heads(
        sent,
        [
            part.reshape(2, chunks, part.shape[0] // (2 * chunks), -1)
            for part, chunks in ((w_out, 1), (w_fc, 4), (w_proj, 4))
        ],
        width,
    )
    out_weight, fc_weight = out_full.reshape(D, D), fc_full.reshape(D, -1)
    proj_weight = proj_full.reshape(-1, D)
    if halo:
        ahead = [(i, i + GROUP) for i in range(ctx_size - GROUP)]
        kv_all = jnp.concatenate(
            [lax.ppermute(kv_all[GROUP - halo :], "ctx", ahead), kv_all], axis=0
        )
    out_wide, out_low, logs = attention_forward(info, q_all, kv_all, lo, halo)
    attended = send_home(out_low)
    resid = inputs + over_rows(attended, out_weight) + out_shift.astype(jnp.float32)
    normed2, norm2_back = jax.vjp(
        norm_layer, resid, norm2_gain.astype(jnp.float32), norm2_shift.astype(jnp.float32)
    )
    normed2_low = normed2.astype(jnp.bfloat16)
    pre_act = jnp.dot(normed2_low, fc_weight, preferred_element_type=jnp.float32) + fc_shift.astype(
        jnp.float32
    )
    activ, gelu_back = jax.vjp(smooth_gate, pre_act)
    activ_low = activ.astype(jnp.bfloat16)
    result = (
        resid
        + jnp.dot(activ_low, proj_weight, preferred_element_type=jnp.float32)
        + proj_shift.astype(jnp.float32)
    )
    valid_rows = (query_pos[None, :] < lengths[:, None]).astype(jnp.float32)
    deviation = (
        result.reshape(seq_count, width, D) - teacher.astype(jnp.float32)
    ) * valid_rows[:, :, None]
    grad_output = deviation.reshape(row_count, D)
    grad_mixed = grad_output.astype(jnp.bfloat16)
    grad_proj_w = over_rows(activ_low, grad_mixed)
    grad_proj_b = jnp.sum(grad_mixed.astype(jnp.float32), axis=0)
    grad_activ = over_lanes(grad_mixed, proj_weight)
    grad_pre = gelu_back(grad_activ)[0].astype(jnp.bfloat16)
    grad_fc_w = over_rows(normed2_low, grad_pre)
    grad_fc_b = jnp.sum(grad_pre.astype(jnp.float32), axis=0)
    grad_normed2 = over_lanes(grad_pre, fc_weight)
    grad_resid_norm, grad_g2, grad_b2 = norm2_back(grad_normed2)
    grad_resid = grad_output + grad_resid_norm
    grad_branch = grad_resid.astype(jnp.bfloat16)
    grad_out_w = jnp.dot(attended, grad_branch, preferred_element_type=jnp.float32)
    grad_out_b = jnp.sum(grad_branch.astype(jnp.float32), axis=0)
    grad_attended = over_lanes(out_weight, grad_branch).astype(jnp.bfloat16)
    grad_all = send_away(grad_attended, width)
    dq, dkv = attention_backward(info, q_all, kv_all, lo, grad_all, out_wide, logs, halo)
    if halo:
        behind = [(i + GROUP, i) for i in range(ctx_size - GROUP)]
        over = lax.ppermute(dkv[:halo].astype(jnp.bfloat16), "ctx", behind)
        dkv = dkv[halo:].at[GROUP - halo :].add(over.astype(jnp.float32))
    grads_t, proj_sum, fc_sum, out_sum = return_heads(
        dq, dkv, [as_terms(grad_proj_w, 4), as_terms(grad_fc_w, 4), as_terms(grad_out_w, 1)]
    )
    grad_projected = grads_t[: 2 * D + VW]
    grad_first = grads_t[2 * D + VW :].T.astype(jnp.float32)
    grad_qkv_w = lax.dot_general(
        normed1_low, grad_projected, (((0,), (1,)), ((), ())), preferred_element_type=jnp.float32
    )
    grad_sums = jnp.sum(grad_projected.astype(jnp.float32), axis=1)
    grad_qv_b = jnp.concatenate([grad_sums[:D], grad_sums[2 * D :]])
    grad_normed1 = lax.dot_general(
        grad_projected, qkv_weight, (((0,), (1,)), ((), ())), preferred_element_type=jnp.float32
    )
    grad_input_norm, grad_g1, grad_b1 = norm1_back(grad_normed1)
    grad_inputs = grad_resid + grad_input_norm
    small_grads = (grad_g1, grad_b1, grad_qv_b, grad_out_b, grad_g2, grad_b2, grad_fc_b, grad_proj_b)
    small_grads = jnp.concatenate(
        [part.reshape(2, -1) for part in small_grads], axis=1
    ).reshape(-1)
    scalars = jnp.stack([jnp.sum(deviation * deviation), jnp.sum(valid_rows)])
    small_grads = jnp.concatenate([small_grads, scalars])
    total_rows = pl.cdiv(small_grads.shape[0], 8 * 128) * 8
    small_grads = jnp.pad(small_grads, (0, total_rows * 128 - small_grads.shape[0]))
    small_all, proj_all, fc_all, out_all, qkv_all = finish_sums(
        small_grads.reshape(total_rows, 128),
        [part.reshape(CHIPS, -1, part.shape[-1]) for part in (proj_sum, fc_sum, out_sum)],
        as_terms(grad_qkv_w, CHIPS),
    )
    small_all = small_all.reshape(-1)
    large = [part.reshape(-1, part.shape[-1]) for part in (qkv_all, out_all, fc_all, proj_all)]
    if groups > 1:
        sets = [[first + GROUP * g for g in range(groups)] for first in range(GROUP)]
        small_all = lax.psum(small_all, "ctx", axis_index_groups=sets)
        large = [
            lax.psum(part.astype(jnp.float32), "ctx", axis_index_groups=sets) for part in large
        ]
    large = [part.astype(jnp.float32) for part in large]
    length_all = sum(small_sizes)
    loss = small_all[2 * length_all] / (small_all[2 * length_all + 1] * D)
    my_small = lax.dynamic_slice_in_dim(
        small_all, lax.axis_index("wsh") * length_all, length_all
    )
    shares, at = [], 0
    for size in small_sizes:
        shares.append(my_small[at : at + size])
        at += size
    return (
        loss,
        result.reshape(seq_count, width, D).astype(jnp.bfloat16),
        grad_inputs.reshape(seq_count, width, D),
        grad_first.reshape(seq_count, width, D - VW),
        shares[0],
        shares[1],
        large[0],
        shares[2],
        large[1],
        shares[3],
        shares[4],
        shares[5],
        large[2],
        shares[6],
        large[3],
        shares[7],
    )


def solution(mesh):
    whole, rows, vector = P("wsh", "ctx", None), P("wsh", None), P("wsh")
    in_specs = (whole, whole, whole, rows, vector) + (
        vector,
        vector,
        rows,
        vector,
        rows,
        vector,
        vector,
        vector,
        rows,
        vector,
        rows,
        vector,
    )
    out_specs = (P(), whole, whole, whole) + in_specs[5:]
    return jax.shard_map(local, mesh=mesh, in_specs=in_specs, out_specs=out_specs, check_vma=False)
```
